32 devices in a mesh: grp: 4 (over x, core), blk: 8 (over z, y).
Axes of the slice: x: 2, y: 2, z: 4, core: 2. Of those that a mesh axis runs over, the one named last changes fastest.
Arguments:
- targets: float32 [16, 262144], P('blk', 'grp'), may hold values from -6 to 6
- sources: float32 [32, 262144], P(('grp', 'blk')), may hold values from -6 to 6
- occupation: int32 [32], P(('grp', 'blk')), may hold values from 1 to 2
- offsets: int32 [4], replicated, may hold values from 0 to 7, as said below
Outputs:
- exchange: float32 [16, 262144], P('blk', 'grp')
The draws below stay inside these ranges and needn't reach their ends.
Inputs may be any that keep to these rules, and one draw needn't show every extreme that they name: The groups' offsets are distinct and the largest is 7.
All inputs are finite; a program needn't handle non-finite values.
Results may differ from the reference program's by a relative error of at most 0.0003.
Values sent between devices are 32-bit elements; how exact they have to be, the bound alone decides.
A program may use at most 128 MiB of HBM per device.

```python
import math
import jax
import jax.numpy as jnp
from jax import lax

NG = 64
CELLS = 262144
TGT_DEV = 2
SRC_DEV = 1
STOPS = 4
GROUPS = 4
CYCLE = 8
TGT = 16
NSRC = 32


def draw_offsets(key, part):
    ordering = jax.random.permutation(key, jnp.arange(CYCLE, dtype=jnp.int32))[:GROUPS]
    return (ordering + (CYCLE - 1 - jnp.max(ordering))).astype(jnp.int32)


def plant(drawn, key, least, top_value):
    shape = drawn.shape
    place = [jax.random.randint(jax.random.fold_in(key, axis), (), 0, shape[axis]) for axis in range(len(shape))]
    drawn = drawn.at[tuple(place)].set(least)
    longest = shape.index(max(shape))
    place[longest] = (place[longest] + 1) % shape[longest]
    return drawn.at[tuple(place)].set(top_value)


def block_levels(own_key, shape, pieces, low, top_value):
    level, own = 1.0, jax.random.fold_in(own_key, 6)
    for axis_at, blocks in pieces:
        heights = jnp.exp(jax.random.uniform(jax.random.fold_in(own, axis_at), (blocks,), jnp.float32, low / len(pieces), top_value / len(pieces)))
        level = level * jnp.repeat(heights, shape[axis_at] // blocks).reshape([-1 if axis == axis_at else 1 for axis in range(len(shape))])
    return level


def centred(rng, dims, spread, bound, split=(), kind=jnp.bfloat16):
    array = spread * jax.random.normal(rng, dims, jnp.float32)
    if split:
        array = array * block_levels(rng, dims, split, -0.22, 0.18)
    return jnp.clip(array, -bound, bound).astype(kind)


def setup_inputs(seed: int = 0) -> dict:
    seeds = jax.random.split(jax.random.key(seed), 5)
    return {
        "targets": centred(seeds[0], (TGT, CELLS), 1.0, 6.0, ((0, 8), (1, 4)), jnp.float32),
        "sources": centred(seeds[1], (NSRC, CELLS), 1.0, 6.0, ((0, 32),), jnp.float32),
        "occupation": plant(jax.random.randint(seeds[2], (NSRC,), 1, 3), jax.random.fold_in(seeds[2], 1), 1, 2).astype(jnp.int32),
        "offsets": draw_offsets(jax.random.fold_in(seeds[4], 71), 0),
    }


box_length = 16.0
screen_square = 0.25

def screened_kernel(grid_size):
    counter = jnp.arange(grid_size, dtype=jnp.int32)
    signed_freq = jnp.where(counter < grid_size // 2, counter, counter - grid_size).astype(jnp.float32)
    wave_number = 2.0 * math.pi * signed_freq / box_length
    wave_square = wave_number * wave_number
    summed = wave_square[:, None, None] + wave_square[None, :, None] + wave_square[None, None, :]
    return 4.0 * math.pi / (summed + screen_square)

def pair_potential(density, kernel_grid):
    lead_shape = density.shape[:-1]
    cube_field = density.reshape(lead_shape + (NG, NG, NG))
    spectrum = jnp.fft.fftn(cube_field, axes=(-3, -2, -1))
    potential = jnp.real(jnp.fft.ifftn(spectrum * kernel_grid, axes=(-3, -2, -1)))
    return potential.astype(jnp.float32).reshape(lead_shape + (CELLS,))

def reference(targets, sources, occupation, offsets):
    scaled = sources * jnp.sqrt(occupation.astype(jnp.float32) * 0.5)[:, None]
    by_block = scaled.reshape(GROUPS, CYCLE, SRC_DEV, CELLS)
    target_blocks = targets.reshape(CYCLE, TGT_DEV, CELLS)
    kernel_grid = screened_kernel(NG)

    def one_block(inputs):
        block_index, target_rows = inputs
        accumulated = jnp.zeros((TGT_DEV, CELLS), jnp.float32)
        for group_index in range(GROUPS):
            for stop_index in range(STOPS):
                source_block = ((block_index - offsets[group_index] - stop_index) % CYCLE).astype(jnp.int32)
                partners = lax.dynamic_index_in_dim(by_block[group_index], source_block, 0, keepdims=False)
                density = target_rows[:, None, :] * partners[None, :, :]
                potential = pair_potential(density, kernel_grid)
                accumulated = accumulated + lax.optimization_barrier(jnp.sum(potential * partners[None, :, :], axis=1))
        return -accumulated
    result = lax.map(one_block, (jnp.arange(CYCLE, dtype=jnp.int32), target_blocks))
    return result.reshape(CYCLE * TGT_DEV, CELLS)
```

```python
import functools
import math

import jax
import jax.numpy as jnp
import numpy as np
from jax import lax
from jax.experimental import pallas as pl
from jax.experimental.pallas import tpu as pltpu
from jax.sharding import PartitionSpec as P

NG = 64
STOPS = 4
LANES = 128

box_length = 16.0
screen_square = 0.25


def split_np(table):
    high = table.astype(jnp.bfloat16)
    low = (table - high.astype(np.float64)).astype(jnp.bfloat16)
    return high, low


def stacked(table):
    high, low = split_np(table)
    return np.concatenate(
        [np.concatenate([high, high], axis=1), np.concatenate([low, low], axis=1)], axis=0
    )


def tables():
    counter = np.arange(NG)
    angle = 2.0 * np.pi * (counter[:, None] * counter[None, :] % NG) / NG
    cas = (np.cos(angle) + np.sin(angle)) / math.sqrt(NG)
    order = np.concatenate([counter[0::2], counter[1::2]])
    along_x = stacked(cas)
    along_y = stacked(cas[:, order])
    back_y = stacked(cas[order, :])
    z_high, z_low = split_np(np.kron(np.eye(4), cas))
    freq = np.where(counter < NG // 2, counter, counter - NG)
    wave = (2.0 * np.pi * freq / box_length) ** 2
    plane = wave[:, None] + np.tile(wave, 2)[None, :] + screen_square
    return along_x, along_y, back_y, z_high, z_low, plane.astype(np.float32), wave.astype(np.float32)


def split(value):
    high = value.astype(jnp.bfloat16)
    low = (value - high.astype(jnp.float32)).astype(jnp.bfloat16)
    return high, low


def left(table, value):
    high, low = split(value)
    both = jnp.dot(
        table, jnp.concatenate([high, low], axis=0), preferred_element_type=jnp.float32
    )
    return both[:NG] + both[NG:]


def right(z_high, z_low, value):
    high, low = split(value)
    dot = functools.partial(jnp.dot, preferred_element_type=jnp.float32)
    return dot(high, z_high) + (dot(low, z_high) + dot(high, z_low))


HALF = NG // 2
XB = 16
YB = 8
CALLS = ((0, 1), (1, 3), (3, 4))


def pair_kernel(count, has_prior, slots, wave, *refs):
    pool = refs[:count]
    refs = refs[count:]
    targets, along_x, along_y, back_y, z_high, z_low, plane = refs[:7]
    refs = refs[7:]
    if has_prior:
        prior, refs = refs[0], refs[1:]
    out, src, field, sems = refs
    ns = src.shape[0]
    xb, yb = XB * 2 // ns, YB * 2 // ns
    width = ns * LANES

    def wide(parts):
        return jnp.concatenate(parts, axis=1) if ns > 1 else parts[0]

    def load(rows):
        return wide([field[s, rows, :] for s in range(ns)])

    def store(rows, v):
        for s in range(ns):
            field[s, rows, :] = v[:, s * LANES : (s + 1) * LANES]

    for s in range(ns):
        for i in range(count):
            @pl.when(slots[s] == i)
            def _():
                pltpu.make_async_copy(pool[i], src.at[s], sems.at[s]).start()
    for s in range(ns):
        pltpu.make_async_copy(pool[0], src.at[s], sems.at[s]).wait()

    first = lax.broadcasted_iota(jnp.int32, (HALF, LANES), 1) < NG

    def interleave(a, b):
        even = jnp.where(first, a, pltpu.roll(b, NG, 1))
        odd = jnp.where(first, pltpu.roll(a, NG, 1), b)
        return even, odd

    def source_rows(s, x):
        v = src[s, pl.ds(pl.multiple_of(x * HALF, HALF), HALF), :]
        even, odd = interleave(v, v)
        return jnp.concatenate([even, odd], axis=0)

    def source_plane(x):
        return wide([source_rows(s, x) for s in range(ns)])

    def forward(step, carry):
        slabs = []
        for k in range(xb):
            x = step * xb + k
            rows = pl.ds(pl.multiple_of(x * HALF, HALF), HALF)
            even, odd = interleave(targets[0, rows, :], targets[1, rows, :])
            t = jnp.concatenate([even, odd], axis=0)
            slabs.append(wide([t] * ns) * source_plane(x))
        lines = right(z_high[:width, :width], z_low[:width, :width], jnp.concatenate(slabs, axis=0))
        for k in range(xb):
            x = step * xb + k
            rows = pl.ds(pl.multiple_of(x * NG, NG), NG)
            store(rows, left(along_y[...], lines[k * NG : (k + 1) * NG]))
        return carry

    def middle(step, carry):
        group = [step * yb + k for k in range(yb)]
        slabs = []
        for y in group:
            rows = pl.ds(y, NG, stride=NG)
            slabs.append(load(rows))
        slabs = [left(along_x[...], v) for v in slabs]
        for k, y in enumerate(group):
            factor = (4.0 * math.pi) / (plane[...] + wave[y])
            slabs[k] = slabs[k] * wide([factor] * ns)
        slabs = [left(along_x[...], v) for v in slabs]
        for y, v in zip(group, slabs):
            rows = pl.ds(y, NG, stride=NG)
            store(rows, v)
        return carry

    def backward(step, carry):
        slabs = []
        for k in range(xb):
            x = step * xb + k
            rows = pl.ds(pl.multiple_of(x * NG, NG), NG)
            slabs.append(left(back_y[...], load(rows)))
        lines = right(z_high[:width, :width], z_low[:width, :width], jnp.concatenate(slabs, axis=0))
        for k in range(xb):
            x = step * xb + k
            v = lines[k * NG : (k + 1) * NG] * source_plane(x)
            v = sum(v[:, s * LANES : (s + 1) * LANES] for s in range(ns))
            a, b = interleave(v[:HALF], v[HALF:])
            rows = pl.ds(pl.multiple_of(x * HALF, HALF), HALF)
            if has_prior:
                out[0, rows, :] = prior[0, rows, :] - a
                out[1, rows, :] = prior[1, rows, :] - b
            else:
                out[0, rows, :] = -a
                out[1, rows, :] = -b
        return carry

    lax.fori_loop(0, NG // xb, forward, 0)
    lax.fori_loop(0, NG // yb, middle, 0)
    lax.fori_loop(0, NG // xb, backward, 0)


def exchange_terms(slots, pool, targets, prior, consts):
    *mats, wave = consts
    rows = targets.shape[1]
    ns = slots.shape[0]
    smem = pl.BlockSpec(memory_space=pltpu.SMEM)
    vmem = pl.BlockSpec(memory_space=pltpu.VMEM)
    anywhere = pl.BlockSpec(memory_space=pl.ANY)
    extra = [] if prior is None else [prior]
    return pl.pallas_call(
        functools.partial(pair_kernel, len(pool), prior is not None),
        out_shape=jax.ShapeDtypeStruct(targets.shape, jnp.float32),
        in_specs=[smem, smem] + [anywhere] * len(pool) + [vmem] * (1 + len(mats) + len(extra)),
        out_specs=vmem,
        scratch_shapes=[
            pltpu.VMEM((ns, rows, LANES), jnp.float32),
            pltpu.VMEM((ns, NG * NG, LANES), jnp.float32),
            pltpu.SemaphoreType.DMA((ns,)),
        ],
        compiler_params=pltpu.CompilerParams(vmem_limit_bytes=40 * 1024 * 1024),
        cost_estimate=pl.CostEstimate(
            flops=10_000_000_000 * ns, bytes_accessed=8_000_000, transcendentals=0
        ),
    )(slots, wave, *pool, targets, *mats, *extra)


CHUNKS = 4
SLOTS = 5
PIECE = 64
BLOCK = 8


def exchange_kernel(
    offsets, wave, src, tgt, along_x, along_y, back_y, z_high, z_low, plane, out,
    held, outbox, give, pool, whole, total, field, near, over, across,
    held_sem, a_sem, inner_sem, outer_sem, give_sem, pool_sem,
    t_send, t_recv, near_send, near_recv, x_send, x_recv,
):
    planes = lax.axis_size("blk") // 2
    half_rows = src.shape[0] // 2
    chunk_rows = half_rows // CHUNKS
    quarter_rows = tgt.shape[1]
    me, grp = lax.axis_index("blk"), lax.axis_index("grp")
    z, y = me // 2, me % 2
    buddy = 2 * z + 1 - y
    x, core = grp // 2, grp % 2
    mate = 2 * x + 1 - core
    cross = 2 * (1 - x) + core
    cross_mate = 2 * (1 - x) + 1 - core
    is_end = (z == 0) | (z == planes - 1)
    is_mid = jnp.logical_not(is_end)
    z_in = 1 + z % 2
    z_out = (planes - 1) * jnp.maximum(z - 1, 0)
    z_far = planes - 1 - z_out
    to_buddy, to_in = {"blk": buddy}, {"blk": 2 * z_in + y}
    to_out = {"blk": 2 * z_out + y}
    to_mate, to_cross = {"grp": mate}, {"grp": cross}

    def remote(a, b, send, recv, device):
        return pltpu.make_async_remote_copy(
            src_ref=a, dst_ref=b, send_sem=send, recv_sem=recv,
            device_id=device, device_id_type=pl.DeviceIdType.MESH,
        )

    barrier = pltpu.get_barrier_semaphore()
    for device in (to_buddy, to_in, to_mate, to_cross):
        pl.semaphore_signal(barrier, inc=1, device_id=device, device_id_type=pl.DeviceIdType.MESH)

    @pl.when(is_mid)
    def _():
        pl.semaphore_signal(barrier, inc=1, device_id=to_out, device_id_type=pl.DeviceIdType.MESH)
        pl.semaphore_wait(barrier, 5)

    @pl.when(is_end)
    def _():
        pl.semaphore_wait(barrier, 4)

    def part(q, base=0):
        return pl.ds(pl.multiple_of(base + q * chunk_rows, chunk_rows), chunk_rows)

    def swap(q):
        return remote(
            src.at[part(q, (1 - y) * half_rows)], held.at[y, part(q)],
            a_sem.at[q], held_sem.at[y, q], to_buddy,
        )

    def inward(s, q):
        at = jnp.where(s < 2, s, 2 * (s - 1))
        to = jnp.where(is_end, 2 + 2 * s, jnp.where(s == 0, 3, s + 4))
        return remote(
            held.at[at, part(q)], held.at[to, part(q)],
            inner_sem.at[s, q], held_sem.at[to, q], to_in,
        )

    def outward(s, q):
        return remote(
            outbox.at[s, part(q)], held.at[2 + s, part(q)],
            outer_sem.at[s, q], held_sem.at[2 + s, q], to_out,
        )

    def handing(k, q):
        return remote(
            give.at[k, part(q)], pool.at[k, part(q, y * half_rows)],
            give_sem.at[k, q], pool_sem.at[k, q], to_buddy,
        )

    def arrived(p, q):
        remote(
            held.at[p, part(q)], held.at[p, part(q)],
            a_sem.at[q], held_sem.at[p, q], to_buddy,
        ).wait_recv()

    def quarter(r, i=None):
        if i is None:
            return pl.ds(pl.multiple_of(r * quarter_rows, quarter_rows), quarter_rows)
        n = quarter_rows // 2
        return pl.ds(pl.multiple_of(r * quarter_rows + i * n, n), n)

    def target_to(n):
        if n == 0:
            a, r, device = tgt, grp, to_mate
        elif n == 1:
            a, r, device = tgt, grp, to_cross
        else:
            a, r, device = whole.at[:, quarter(cross)], cross, to_mate
        return remote(a, whole.at[:, quarter(r)], t_send.at[n], t_recv.at[n], device)

    def sum_to_mate(n, i):
        r = jnp.where(n == 0, cross_mate, mate)
        return remote(
            total.at[:, quarter(r, i)], near.at[n, :, quarter(0, i)],
            near_send.at[n, i], near_recv.at[n, i], to_mate,
        )

    def sum_to_cross(i):
        return remote(
            across.at[:, quarter(0, i)], over.at[:, quarter(0, i)],
            x_send.at[i], x_recv.at[i], to_cross,
        )

    for q in range(CHUNKS):
        swap(q).start()
    target_to(0).start()
    target_to(1).start()

    def keep(i, carry):
        rows = pl.ds(pl.multiple_of(i * PIECE, PIECE), PIECE)
        at = pl.ds(pl.multiple_of(y * half_rows + i * PIECE, PIECE), PIECE)
        held[y, rows, :] = src[at, :]
        return carry

    lax.fori_loop(0, half_rows // PIECE, keep, 0)

    @pl.when(y == 0)
    def _():
        for q in range(CHUNKS):
            inward(0, q).start()

    off = offsets[grp]

    def flag(value):
        return value.astype(jnp.int32)

    count = 2 * planes

    def needs(b, c):
        return flag(lax.rem(b - c - off + 2 * count, count) < STOPS)

    end = jnp.where(is_end, z, z_out)
    line = []
    for d in range(1, planes):
        p = jnp.where(end == 0, d, planes - 1 - d)
        line += [2 * p, 2 * p + 1]
    skip = jnp.int32(0)
    found = jnp.int32(0)
    for i, c in enumerate(line):
        spare = (1 - found) * (1 - needs(2 * end, c)) * (1 - needs(2 * end + 1, c))
        skip = skip + i * spare
        found = found + spare
    mid_ids = [2 * z, 2 * z + 1, 2 * z_out, 2 * z_in, 2 * z_out + 1, 2 * z_in + 1, 2 * z_far, 2 * z_far + 1]
    end_ids = [2 * z, 2 * z + 1]
    end_ids += [jnp.where(s < skip, line[s], line[s + 1]) for s in range(SLOTS)]

    def places(b):
        rank = jnp.int32(0)
        at = [jnp.int32(0)] * STOPS
        for p, c in enumerate(mid_ids):
            if p < len(end_ids):
                want = needs(b, jnp.where(is_end, end_ids[p], c))
            else:
                want = jnp.where(is_end, 0, needs(b, c))
            for k in range(STOPS):
                at[k] = at[k] + (p - k) * want * flag(rank == k)
            rank = rank + want
        return at

    my_places, buddy_places = places(me), places(buddy)

    def pick(places, k):
        return sum(jnp.where(k == i, places[i], 0) for i in range(STOPS))

    def send_out(s, q):
        first = jnp.where(s < 2, s, jnp.where(s == 2, 3, s + 2))
        second = jnp.where(s + 1 < 2, s + 1, jnp.where(s + 1 == 2, 3, s + 3))
        for i in range(chunk_rows // PIECE):
            rows = pl.ds(q * chunk_rows + i * PIECE, PIECE)
            outbox[s, rows, :] = jnp.where(s < skip, held[first, rows, :], held[second, rows, :])
        outward(s, q).start()

    def choose(k, q):
        mine, other = pick(my_places, k), pick(buddy_places, k)
        short = flag(is_end)
        for i in range(chunk_rows // PIECE):
            rows = pl.ds(q * chunk_rows + i * PIECE, PIECE)
            a = b = held[k, rows, :]
            for j in range(1, STOPS + 1):
                at = k + j - (short if j == STOPS else 0)
                v = held[at, rows, :]
                a = jnp.where(mine == j, v, a)
                b = jnp.where(other == j, v, b)
            give[k, rows, :] = b
            at = pl.multiple_of(y * half_rows + q * chunk_rows + i * PIECE, PIECE)
            pool[k, pl.ds(at, PIECE), :] = a
        handing(k, q).start()

    for q in range(CHUNKS):
        arrived(1 - y, q)

        @pl.when(y == 1)
        def _():
            inward(0, q).start()

        inward(1, q).start()

        @pl.when(is_mid)
        def _():
            send_out(0, q)

    def own(i, carry):
        rows = pl.ds(pl.multiple_of(i * PIECE, PIECE), PIECE)
        at = pl.ds(pl.multiple_of(grp * quarter_rows + i * PIECE, PIECE), PIECE)
        whole[:, at, :] = tgt[:, rows, :]
        return carry

    lax.fori_loop(0, quarter_rows // PIECE, own, 0)

    def target_from(n):
        r = (mate, cross, cross_mate)[n]
        remote(
            tgt, whole.at[:, quarter(r)], t_send.at[n], t_recv.at[n], to_mate
        ).wait_recv()

    target_from(1)
    target_to(2).start()
    target_from(0)
    target_from(2)

    first = lax.broadcasted_iota(jnp.int32, (HALF, LANES), 1) < NG

    def interleave(a, b):
        even = jnp.where(first, a, pltpu.roll(b, NG, 1))
        odd = jnp.where(first, pltpu.roll(a, NG, 1), b)
        return even, odd

    def source_plane(k, at):
        v = pool[k, pl.ds(pl.multiple_of(at * HALF, HALF), HALF), :]
        even, odd = interleave(v, v)
        return jnp.concatenate([even, odd], axis=0)

    z_table = (z_high[:LANES, :LANES], z_low[:LANES, :LANES])

    def forward(k, base, n):
        slabs = []
        for i in range(n):
            at = base + i
            rows = pl.ds(pl.multiple_of(at * HALF, HALF), HALF)
            even, odd = interleave(whole[0, rows, :], whole[1, rows, :])
            slabs.append(jnp.concatenate([even, odd], axis=0) * source_plane(k, at))
        lines = right(*z_table, jnp.concatenate(slabs, axis=0))
        for i in range(n):
            rows = pl.ds(pl.multiple_of((base + i) * NG, NG), NG)
            field[rows, :] = left(along_y[...], lines[i * NG : (i + 1) * NG])

    def middle(step, carry):
        group = [step * YB + i for i in range(YB)]
        slabs = [left(along_x[...], field[pl.ds(i, NG, stride=NG), :]) for i in group]
        for i, at in enumerate(group):
            slabs[i] = slabs[i] * ((4.0 * math.pi) / (plane[...] + wave[at]))
        slabs = [left(along_x[...], v) for v in slabs]
        for at, v in zip(group, slabs):
            field[pl.ds(at, NG, stride=NG), :] = v
        return carry

    def backward(k, base, n):
        slabs = []
        for i in range(n):
            rows = pl.ds(pl.multiple_of((base + i) * NG, NG), NG)
            slabs.append(left(back_y[...], field[rows, :]))
        lines = right(*z_table, jnp.concatenate(slabs, axis=0))
        for i in range(n):
            v = lines[i * NG : (i + 1) * NG] * source_plane(k, base + i)
            a, b = interleave(v[:HALF], v[HALF:])
            rows = pl.ds(pl.multiple_of((base + i) * HALF, HALF), HALF)
            total[0, rows, :] = jnp.where(k == 0, 0.0, total[0, rows, :]) - a
            total[1, rows, :] = jnp.where(k == 0, 0.0, total[1, rows, :]) - b

    half_planes = NG // 2
    per_chunk = half_planes // CHUNKS

    def forward_own(k):
        def body(q, carry):
            forward(k, y * half_planes + q * per_chunk, per_chunk)
            return carry

        lax.fori_loop(0, CHUNKS, body, 0)

    def forward_other(k):
        def body(q, carry):
            remote(
                give.at[k, part(q)], pool.at[k, part(q, (1 - y) * half_rows)],
                give_sem.at[k, q], pool_sem.at[k, q], to_buddy,
            ).wait_recv()
            forward(k, (1 - y) * half_planes + q * per_chunk, per_chunk)
            return carry

        lax.fori_loop(0, CHUNKS, body, 0)

    def near_from(n, i):
        remote(
            over.at[:, quarter(0, i)], near.at[n, :, quarter(0, i)],
            near_send.at[n, i], near_recv.at[n, i], to_mate,
        ).wait_recv()

    quarter_planes = NG // 4
    blocks = quarter_planes // 2

    def back(k):
        def body(j, carry):
            turn, i = j // 2, j % 2
            r = jnp.where(
                turn == 0, cross_mate, jnp.where(turn == 1, cross, jnp.where(turn == 2, mate, grp))
            )
            backward(k, r * quarter_planes + i * blocks, blocks)
            last = k == STOPS - 1

            @pl.when(last & (turn % 2 == 0))
            def _():
                sum_to_mate(turn // 2, i).start()

            @pl.when(last & (turn == 1))
            def _():
                near_from(0, i)
                across[:, quarter(0, i), :] = total[:, quarter(cross, i), :] + near[0, :, quarter(0, i), :]
                sum_to_cross(i).start()

            return carry

        lax.fori_loop(0, 8, body, 0)

    def step(t, carry):
        def comm(q):
            @pl.when(is_end & (t < SLOTS))
            def _():
                arrived(2 + t, q)

            @pl.when(is_mid & (t < SLOTS - 1))
            def _():
                arrived(jnp.where(t == 0, 3, t + 4), q)

                @pl.when(t < 2)
                def _():
                    arrived(2 + 2 * t, q)
                    inward(t + 2, q).start()

                send_out(t + 1, q)

            @pl.when((t >= 1) & (t < SLOTS))
            def _():
                choose(t - 1, q)

        comm(0)

        @pl.when(t >= 2)
        def _():
            forward_other(t - 2)

        comm(1)

        @pl.when(t >= 2)
        def _():
            lax.fori_loop(0, NG // YB, middle, 0)

        comm(2)

        @pl.when(t >= 2)
        def _():
            back(t - 2)

        comm(3)

        @pl.when((t >= 1) & (t < SLOTS))
        def _():
            forward_own(t - 1)

        return carry

    lax.fori_loop(0, STOPS + 2, step, 0)

    for i in range(2):
        near_from(1, i)
        remote(
            across.at[:, quarter(0, i)], over.at[:, quarter(0, i)],
            x_send.at[i], x_recv.at[i], to_cross,
        ).wait_recv()
        out[:, quarter(0, i), :] = (
            total[:, quarter(grp, i), :] + near[1, :, quarter(0, i), :] + over[:, quarter(0, i), :]
        )

    for n in range(3):
        target_to(n).wait_send()
    for i in range(2):
        sum_to_cross(i).wait_send()
        for n in range(2):
            sum_to_mate(n, i).wait_send()

    def drain(q, carry):
        swap(q).wait_send()
        for k in range(STOPS):
            handing(k, q).wait_send()
        for s in range(2):
            inward(s, q).wait_send()

        @pl.when(is_mid)
        def _():
            for s in range(2, 4):
                inward(s, q).wait_send()
            for s in range(SLOTS):
                outward(s, q).wait_send()

        return carry

    lax.fori_loop(0, CHUNKS, drain, 0)


def plane_exchange(offsets, scaled, quarter, consts):
    *mats, wave = consts
    rows = scaled.shape[0]
    half = rows // 2
    targets, part = quarter.shape[:2]
    smem = pl.BlockSpec(memory_space=pltpu.SMEM)
    vmem = pl.BlockSpec(memory_space=pltpu.VMEM)
    dma = pltpu.SemaphoreType.DMA
    box = functools.partial(pltpu.VMEM, dtype=jnp.float32)
    return pl.pallas_call(
        exchange_kernel,
        out_shape=jax.ShapeDtypeStruct(quarter.shape, jnp.float32),
        in_specs=[smem, smem] + [vmem] * (2 + len(mats)),
        out_specs=vmem,
        scratch_shapes=[
            box((8, half, LANES)),
            box((SLOTS, half, LANES)),
            box((STOPS, half, LANES)),
            box((STOPS, rows, LANES)),
            box((targets, rows, LANES)),
            box((targets, rows, LANES)),
            box((NG * NG, LANES)),
            box((2, targets, part, LANES)),
            box((targets, part, LANES)),
            box((targets, part, LANES)),
            dma((8, CHUNKS)),
            dma((CHUNKS,)),
            dma((4, CHUNKS)),
            dma((SLOTS, CHUNKS)),
            dma((STOPS, CHUNKS)),
            dma((STOPS, CHUNKS)),
            dma((3,)),
            dma((3,)),
            dma((2, 2)),
            dma((2, 2)),
            dma((2,)),
            dma((2,)),
        ],
        compiler_params=pltpu.CompilerParams(
            vmem_limit_bytes=48 * 1024 * 1024, collective_id=0, has_side_effects=True
        ),
        cost_estimate=pl.CostEstimate(
            flops=40_000_000_000, bytes_accessed=8_000_000, transcendentals=0
        ),
    )(offsets, wave, scaled, quarter, *mats)


def ring_order(count):
    return list(range(0, count, 2)) + list(range(1, count, 2))[::-1]


def arrival(count):
    order = ring_order(count)
    place = [order.index(i) for i in range(count)]
    worst = [0] * STOPS
    for b in range(count):
        for off in range(count):
            steps = []
            for k in range(STOPS):
                d = (place[b] - place[(b - off - k) % count]) % count
                steps.append(min(d, count - d))
            worst = [max(w, s) for w, s in zip(worst, sorted(steps))]
    return worst


def partner(value, axis, bit):
    return lax.ppermute(value, axis, [(i, i ^ bit) for i in range(lax.axis_size(axis))])


def gather_rows(quarter, axis):
    me = lax.axis_index(axis)
    count = lax.axis_size(axis)
    parts = {0: quarter}
    bit = count // 2
    while bit:
        for key, value in list(parts.items()):
            parts[key ^ bit] = partner(value, axis, bit)
        bit //= 2
    ordered = []
    keys = sorted(parts)
    level = [parts[k] for k in keys]
    bit = 1
    while bit < count:
        swap = (me // bit) % 2 == 1
        merged = []
        for i in range(0, len(level), 2):
            a, b = level[i], level[i + 1]
            merged.append(
                jnp.concatenate([jnp.where(swap, b, a), jnp.where(swap, a, b)], axis=1)
            )
        level = merged
        bit *= 2
    return level[0]


def scatter_rows(total, axis):
    me = lax.axis_index(axis)
    count = lax.axis_size(axis)
    targets, rows, lanes = total.shape
    value = total.reshape((targets, count, rows // count, lanes))
    bit = 1
    while bit < count:
        mine = (me // bit) % 2 == 1
        pairs = value.reshape((targets, value.shape[1] // 2, 2) + value.shape[2:])
        low, high = pairs[:, :, 0], pairs[:, :, 1]
        value = jnp.where(mine, high, low) + partner(jnp.where(mine, low, high), axis, bit)
        bit *= 2
    return value[:, 0]


def local(targets, sources, occupation, offsets):
    count = lax.axis_size("blk")
    target_count, cells = targets.shape[0], sources.shape[1]
    consts = [jnp.asarray(v) for v in tables()]
    scaled = sources * jnp.sqrt(occupation.astype(jnp.float32) * 0.5)[:, None]
    scaled = scaled.reshape(cells // LANES, LANES)
    quarter = targets.reshape(target_count, targets.shape[1] // LANES, LANES)
    if count == 2 * STOPS and lax.axis_size("grp") == 4:
        return plane_exchange(offsets, scaled, quarter, consts).reshape(targets.shape)
    whole = gather_rows(quarter, "grp")

    order = ring_order(count)
    up = [(order[i], order[(i + 1) % count]) for i in range(count)]
    down = [(b, a) for a, b in up]
    worst = arrival(count)
    pool = [scaled]
    ahead = behind = scaled
    for step in range(1, count // 2 + 1):
        if step < count // 2:
            ahead = lax.ppermute(ahead, "blk", up)
            behind = lax.ppermute(behind, "blk", down)
            pool += [ahead, behind]
        else:
            half = scaled.shape[0] // 2
            upper = lax.ppermute(ahead[:half], "blk", up)
            lower = lax.ppermute(behind[half:], "blk", down)
            pool += [jnp.concatenate([upper, lower], axis=0)]

    place = np.zeros(count, np.int32)
    place[order] = np.arange(count)
    place = jnp.asarray(place)
    me = lax.axis_index("blk")
    offset = lax.dynamic_index_in_dim(offsets, lax.axis_index("grp"), 0, keepdims=False)
    block = (me - offset - jnp.arange(STOPS, dtype=jnp.int32)) % count
    back = (place[me] - place[block]) % count
    slot = jnp.where(
        back == 0, 0, jnp.where(back <= count // 2, 2 * back - 1, 2 * (count - back))
    ).astype(jnp.int32)
    rank = jnp.sum((slot[None, :] < slot[:, None]).astype(jnp.int32), axis=1)
    ranked = jnp.sum(
        jnp.where(rank[None, :] == jnp.arange(STOPS)[:, None], slot[None, :], 0), axis=1
    ).astype(jnp.int32)

    total = None
    for first, end in CALLS:
        there = pool[: 2 * worst[end - 1] + 1]
        total = exchange_terms(ranked[first:end], there, whole, total, consts)
    return scatter_rows(total, "grp").reshape(targets.shape)


def solution(mesh):
    in_specs = (P("blk", "grp"), P(("grp", "blk"), None), P(("grp", "blk")), P())
    out_specs = P("blk", "grp")
    return jax.shard_map(local, mesh=mesh, in_specs=in_specs, out_specs=out_specs, check_vma=False)
```

```python
import functools
import math

import jax
import jax.numpy as jnp
import numpy as np
from jax import lax
from jax.experimental import pallas as pl
from jax.experimental.pallas import tpu as pltpu
from jax.sharding import PartitionSpec as P

NG = 64
STOPS = 4
LANES = 128

box_length = 16.0
screen_square = 0.25


def split_np(table):
    high = table.astype(jnp.bfloat16)
    low = (table - high.astype(np.float64)).astype(jnp.bfloat16)
    return high, low


def stacked(table):
    high, low = split_np(table)
    return np.concatenate(
        [np.concatenate([high, high], axis=1), np.concatenate([low, low], axis=1)], axis=0
    )


def tables():
    counter = np.arange(NG)
    angle = 2.0 * np.pi * (counter[:, None] * counter[None, :] % NG) / NG
    cas = (np.cos(angle) + np.sin(angle)) / math.sqrt(NG)
    order = np.concatenate([counter[0::2], counter[1::2]])
    along_x = stacked(cas)
    along_y = stacked(cas[:, order])
    back_y = stacked(cas[order, :])
    z_high, z_low = split_np(np.kron(np.eye(4), cas))
    freq = np.where(counter < NG // 2, counter, counter - NG)
    wave = (2.0 * np.pi * freq / box_length) ** 2
    plane = wave[:, None] + np.tile(wave, 2)[None, :] + screen_square
    return along_x, along_y, back_y, z_high, z_low, plane.astype(np.float32), wave.astype(np.float32)


def split(value):
    high = value.astype(jnp.bfloat16)
    low = (value - high.astype(jnp.float32)).astype(jnp.bfloat16)
    return high, low


def left(table, value):
    high, low = split(value)
    both = jnp.dot(
        table, jnp.concatenate([high, low], axis=0), preferred_element_type=jnp.float32
    )
    return both[:NG] + both[NG:]


def right(z_high, z_low, value):
    high, low = split(value)
    dot = functools.partial(jnp.dot, preferred_element_type=jnp.float32)
    return dot(high, z_high) + (dot(low, z_high) + dot(high, z_low))


HALF = NG // 2
XB = 16
YB = 8
CALLS = ((0, 1), (1, 3), (3, 4))


def pair_kernel(count, has_prior, slots, wave, *refs):
    pool = refs[:count]
    refs = refs[count:]
    targets, along_x, along_y, back_y, z_high, z_low, plane = refs[:7]
    refs = refs[7:]
    if has_prior:
        prior, refs = refs[0], refs[1:]
    out, src, field, sems = refs
    ns = src.shape[0]
    xb, yb = XB * 2 // ns, YB * 2 // ns
    width = ns * LANES

    def wide(parts):
        return jnp.concatenate(parts, axis=1) if ns > 1 else parts[0]

    def load(rows):
        return wide([field[s, rows, :] for s in range(ns)])

    def store(rows, v):
        for s in range(ns):
            field[s, rows, :] = v[:, s * LANES : (s + 1) * LANES]

    for s in range(ns):
        for i in range(count):
            @pl.when(slots[s] == i)
            def _():
                pltpu.make_async_copy(pool[i], src.at[s], sems.at[s]).start()
    for s in range(ns):
        pltpu.make_async_copy(pool[0], src.at[s], sems.at[s]).wait()

    first = lax.broadcasted_iota(jnp.int32, (HALF, LANES), 1) < NG

    def interleave(a, b):
        even = jnp.where(first, a, pltpu.roll(b, NG, 1))
        odd = jnp.where(first, pltpu.roll(a, NG, 1), b)
        return even, odd

    def source_rows(s, x):
        v = src[s, pl.ds(pl.multiple_of(x * HALF, HALF), HALF), :]
        even, odd = interleave(v, v)
        return jnp.concatenate([even, odd], axis=0)

    def source_plane(x):
        return wide([source_rows(s, x) for s in range(ns)])

    def forward(step, carry):
        slabs = []
        for k in range(xb):
            x = step * xb + k
            rows = pl.ds(pl.multiple_of(x * HALF, HALF), HALF)
            even, odd = interleave(targets[0, rows, :], targets[1, rows, :])
            t = jnp.concatenate([even, odd], axis=0)
            slabs.append(wide([t] * ns) * source_plane(x))
        lines = right(z_high[:width, :width], z_low[:width, :width], jnp.concatenate(slabs, axis=0))
        for k in range(xb):
            x = step * xb + k
            rows = pl.ds(pl.multiple_of(x * NG, NG), NG)
            store(rows, left(along_y[...], lines[k * NG : (k + 1) * NG]))
        return carry

    def middle(step, carry):
        group = [step * yb + k for k in range(yb)]
        slabs = []
        for y in group:
            rows = pl.ds(y, NG, stride=PITCH)
            slabs.append(load(rows))
        slabs = [left(along_x[...], v) for v in slabs]
        for k, y in enumerate(group):
            factor = (4.0 * math.pi) / (plane[...] + wave[y])
            slabs[k] = slabs[k] * wide([factor] * ns)
        slabs = [left(along_x[...], v) for v in slabs]
        for y, v in zip(group, slabs):
            rows = pl.ds(y, NG, stride=PITCH)
            store(rows, v)
        return carry

    def backward(step, carry):
        slabs = []
        for k in range(xb):
            x = step * xb + k
            rows = pl.ds(pl.multiple_of(x * NG, NG), NG)
            slabs.append(left(back_y[...], load(rows)))
        lines = right(z_high[:width, :width], z_low[:width, :width], jnp.concatenate(slabs, axis=0))
        for k in range(xb):
            x = step * xb + k
            v = lines[k * NG : (k + 1) * NG] * source_plane(x)
            v = sum(v[:, s * LANES : (s + 1) * LANES] for s in range(ns))
            a, b = interleave(v[:HALF], v[HALF:])
            rows = pl.ds(pl.multiple_of(x * HALF, HALF), HALF)
            if has_prior:
                out[0, rows, :] = prior[0, rows, :] - a
                out[1, rows, :] = prior[1, rows, :] - b
            else:
                out[0, rows, :] = -a
                out[1, rows, :] = -b
        return carry

    lax.fori_loop(0, NG // xb, forward, 0)
    lax.fori_loop(0, NG // yb, middle, 0)
    lax.fori_loop(0, NG // xb, backward, 0)


def exchange_terms(slots, pool, targets, prior, consts):
    *mats, wave = consts
    rows = targets.shape[1]
    ns = slots.shape[0]
    smem = pl.BlockSpec(memory_space=pltpu.SMEM)
    vmem = pl.BlockSpec(memory_space=pltpu.VMEM)
    anywhere = pl.BlockSpec(memory_space=pl.ANY)
    extra = [] if prior is None else [prior]
    return pl.pallas_call(
        functools.partial(pair_kernel, len(pool), prior is not None),
        out_shape=jax.ShapeDtypeStruct(targets.shape, jnp.float32),
        in_specs=[smem, smem] + [anywhere] * len(pool) + [vmem] * (1 + len(mats) + len(extra)),
        out_specs=vmem,
        scratch_shapes=[
            pltpu.VMEM((ns, rows, LANES), jnp.float32),
            pltpu.VMEM((ns, NG * NG, LANES), jnp.float32),
            pltpu.SemaphoreType.DMA((ns,)),
        ],
        compiler_params=pltpu.CompilerParams(vmem_limit_bytes=40 * 1024 * 1024),
        cost_estimate=pl.CostEstimate(
            flops=10_000_000_000 * ns, bytes_accessed=8_000_000, transcendentals=0
        ),
    )(slots, wave, *pool, targets, *mats, *extra)


CHUNKS = 4
SLOTS = 5
PIECE = 64
FPLANES = 32
BPLANES = 32
MROWS = 32
PITCH = 72
PREP = 4


def exchange_kernel(
    offsets, wave, src, tgt, along_x, along_y, back_y, z_table, plane, out,
    held, outbox, give, pool, whole, paired, factor, doubled, total, field, near, over, across,
    held_sem, a_sem, inner_sem, outer_sem, give_sem, pool_sem,
    t_send, t_recv, near_send, near_recv, x_send, x_recv,
):
    planes = lax.axis_size("blk") // 2
    half_rows = src.shape[0] // 2
    chunk_rows = half_rows // CHUNKS
    quarter_rows = tgt.shape[1]
    me, grp = lax.axis_index("blk"), lax.axis_index("grp")
    z, y = me // 2, me % 2
    buddy = 2 * z + 1 - y
    x, core = grp // 2, grp % 2
    mate = 2 * x + 1 - core
    cross = 2 * (1 - x) + core
    cross_mate = 2 * (1 - x) + 1 - core
    is_end = (z == 0) | (z == planes - 1)
    is_mid = jnp.logical_not(is_end)
    z_in = 1 + z % 2
    z_out = (planes - 1) * jnp.maximum(z - 1, 0)
    z_far = planes - 1 - z_out
    to_buddy, to_in = {"blk": buddy}, {"blk": 2 * z_in + y}
    to_out = {"blk": 2 * z_out + y}
    to_mate, to_cross = {"grp": mate}, {"grp": cross}

    def remote(a, b, send, recv, device):
        return pltpu.make_async_remote_copy(
            src_ref=a, dst_ref=b, send_sem=send, recv_sem=recv,
            device_id=device, device_id_type=pl.DeviceIdType.MESH,
        )

    barrier = pltpu.get_barrier_semaphore()
    for device in (to_buddy, to_in, to_mate, to_cross):
        pl.semaphore_signal(barrier, inc=1, device_id=device, device_id_type=pl.DeviceIdType.MESH)

    @pl.when(is_mid)
    def _():
        pl.semaphore_signal(barrier, inc=1, device_id=to_out, device_id_type=pl.DeviceIdType.MESH)
        pl.semaphore_wait(barrier, 5)

    @pl.when(is_end)
    def _():
        pl.semaphore_wait(barrier, 4)

    def part(q, base=0):
        return pl.ds(pl.multiple_of(base + q * chunk_rows, chunk_rows), chunk_rows)

    def swap(q):
        return remote(
            src.at[part(q, (1 - y) * half_rows)], held.at[y, part(q)],
            a_sem.at[q], held_sem.at[y, q], to_buddy,
        )

    def inward(s, q):
        at = jnp.where(s < 2, s, 2 * (s - 1))
        to = jnp.where(is_end, 2 + 2 * s, jnp.where(s == 0, 3, s + 4))
        return remote(
            held.at[at, part(q)], held.at[to, part(q)],
            inner_sem.at[s, q], held_sem.at[to, q], to_in,
        )

    def outward(s, q):
        return remote(
            outbox.at[s, part(q)], held.at[2 + s, part(q)],
            outer_sem.at[s, q], held_sem.at[2 + s, q], to_out,
        )

    def handing(k, q):
        return remote(
            give.at[k, part(q)], pool.at[k, part(q, y * half_rows)],
            give_sem.at[k, q], pool_sem.at[k, q], to_buddy,
        )

    def arrived(p, q):
        remote(
            held.at[p, part(q)], held.at[p, part(q)],
            a_sem.at[q], held_sem.at[p, q], to_buddy,
        ).wait_recv()

    def quarter(r):
        return pl.ds(pl.multiple_of(r * quarter_rows, quarter_rows), quarter_rows)

    def share(r, i):
        return pl.ds(pl.multiple_of((2 * r + i) * quarter_rows, quarter_rows), quarter_rows)

    def target_to(n):
        if n == 0:
            a, r, device = tgt, grp, to_mate
        elif n == 1:
            a, r, device = tgt, grp, to_cross
        else:
            a, r, device = whole.at[:, quarter(cross)], cross, to_mate
        return remote(a, whole.at[:, quarter(r)], t_send.at[n], t_recv.at[n], device)

    def sum_to_mate(n, i):
        r = jnp.where(n == 0, cross_mate, mate)
        return remote(
            total.at[share(r, i)], near.at[n, share(0, i)],
            near_send.at[n, i], near_recv.at[n, i], to_mate,
        )

    def sum_to_cross(i):
        return remote(
            across.at[share(0, i)], over.at[share(0, i)],
            x_send.at[i], x_recv.at[i], to_cross,
        )

    first = lax.broadcasted_iota(jnp.int32, (HALF, LANES), 1) < NG

    def interleave(a, b):
        even = jnp.where(first, a, pltpu.roll(b, NG, 1))
        odd = jnp.where(first, pltpu.roll(a, NG, 1), b)
        return even, odd

    def rows_of(at, n=1):
        return pl.ds(pl.multiple_of(at * NG, NG), n * NG)

    def lines_of(at):
        return pl.ds(pl.multiple_of(at * HALF, HALF), HALF)

    def along_z(value):
        high, low = split(value)
        both = jnp.dot(
            jnp.concatenate([high, low], axis=1), z_table[...], preferred_element_type=jnp.float32
        )
        return both[:, :LANES] + both[:, LANES:]

    def rotate(table, values):
        out = []
        for i in range(0, len(values), 2):
            both = left(table[...], jnp.concatenate(values[i : i + 2], axis=1))
            out += [both[:, :LANES], both[:, LANES:]]
        return out

    def prepare(step, carry):
        for i in range(PREP):
            at = step * PREP + i
            even, odd = interleave(whole[0, lines_of(at), :], whole[1, lines_of(at), :])
            paired[rows_of(at), :] = jnp.concatenate([even, odd], axis=0)
        return carry

    def weigh(step, carry):
        for i in range(PREP):
            at = step * PREP + i
            factor[rows_of(at), :] = (4.0 * math.pi) / (plane[...] + wave[at])
        return carry

    def forward(k, base):
        slabs = []
        for i in range(FPLANES):
            at = base + i
            v = pool[k, lines_of(at), :]
            even, odd = interleave(v, v)
            v = jnp.concatenate([even, odd], axis=0)
            doubled[rows_of(at), :] = v
            slabs.append(paired[rows_of(at), :] * v)
        lines = along_z(jnp.concatenate(slabs, axis=0))
        slabs = rotate(along_y, [lines[i * NG : (i + 1) * NG] for i in range(FPLANES)])
        for i, v in enumerate(slabs):
            field[pl.ds(pl.multiple_of(base * PITCH, 8) + i * PITCH, NG), :] = v

    def middle(step, carry):
        group = [step * MROWS + i for i in range(MROWS)]
        slabs = rotate(along_x, [field[pl.ds(at, NG, stride=PITCH), :] for at in group])
        slabs = [v * factor[rows_of(at), :] for at, v in zip(group, slabs)]
        slabs = rotate(along_x, slabs)
        for at, v in zip(group, slabs):
            field[pl.ds(at, NG, stride=PITCH), :] = v
        return carry

    def backward(k, base):
        slabs = rotate(back_y, [
            field[pl.ds(pl.multiple_of(base * PITCH, 8) + i * PITCH, NG), :] for i in range(BPLANES)
        ])
        lines = along_z(jnp.concatenate(slabs, axis=0))
        for i in range(BPLANES):
            rows = rows_of(base + i)
            v = lines[i * NG : (i + 1) * NG] * doubled[rows, :]
            total[rows, :] = jnp.where(k == 0, 0.0, total[rows, :]) - v

    for q in range(CHUNKS):
        swap(q).start()
    target_to(0).start()
    target_to(1).start()

    def keep(i, carry):
        rows = pl.ds(pl.multiple_of(i * PIECE, PIECE), PIECE)
        at = pl.ds(pl.multiple_of(y * half_rows + i * PIECE, PIECE), PIECE)
        held[y, rows, :] = src[at, :]
        return carry

    lax.fori_loop(0, half_rows // PIECE, keep, 0)

    @pl.when(y == 0)
    def _():
        for q in range(CHUNKS):
            inward(0, q).start()

    off = offsets[grp]

    def flag(value):
        return value.astype(jnp.int32)

    count = 2 * planes

    def needs(b, c):
        return flag(lax.rem(b - c - off + 2 * count, count) < STOPS)

    end = jnp.where(is_end, z, z_out)
    line = []
    for d in range(1, planes):
        p = jnp.where(end == 0, d, planes - 1 - d)
        line += [2 * p, 2 * p + 1]
    skip = jnp.int32(0)
    found = jnp.int32(0)
    for i, c in enumerate(line):
        spare = (1 - found) * (1 - needs(2 * end, c)) * (1 - needs(2 * end + 1, c))
        skip = skip + i * spare
        found = found + spare
    mid_ids = [2 * z, 2 * z + 1, 2 * z_out, 2 * z_in, 2 * z_out + 1, 2 * z_in + 1, 2 * z_far, 2 * z_far + 1]
    end_ids = [2 * z, 2 * z + 1]
    end_ids += [jnp.where(s < skip, line[s], line[s + 1]) for s in range(SLOTS)]

    def places(b):
        rank = jnp.int32(0)
        at = [jnp.int32(0)] * STOPS
        for p, c in enumerate(mid_ids):
            if p < len(end_ids):
                want = needs(b, jnp.where(is_end, end_ids[p], c))
            else:
                want = jnp.where(is_end, 0, needs(b, c))
            for k in range(STOPS):
                at[k] = at[k] + (p - k) * want * flag(rank == k)
            rank = rank + want
        return at

    my_places, buddy_places = places(me), places(buddy)

    def pick(places, k):
        return sum(jnp.where(k == i, places[i], 0) for i in range(STOPS))

    def send_out(s, q):
        first = jnp.where(s < 2, s, jnp.where(s == 2, 3, s + 2))
        second = jnp.where(s + 1 < 2, s + 1, jnp.where(s + 1 == 2, 3, s + 3))
        for i in range(chunk_rows // PIECE):
            rows = pl.ds(q * chunk_rows + i * PIECE, PIECE)
            outbox[s, rows, :] = jnp.where(s < skip, held[first, rows, :], held[second, rows, :])
        outward(s, q).start()

    def choose(k, q):
        mine, other = pick(my_places, k), pick(buddy_places, k)
        short = flag(is_end)
        for i in range(chunk_rows // PIECE):
            rows = pl.ds(q * chunk_rows + i * PIECE, PIECE)
            a = b = held[k, rows, :]
            for j in range(1, STOPS + 1):
                at = k + j - (short if j == STOPS else 0)
                v = held[at, rows, :]
                a = jnp.where(mine == j, v, a)
                b = jnp.where(other == j, v, b)
            give[k, rows, :] = b
            at = pl.multiple_of(y * half_rows + q * chunk_rows + i * PIECE, PIECE)
            pool[k, pl.ds(at, PIECE), :] = a
        handing(k, q).start()

    lax.fori_loop(0, NG // PREP, weigh, 0)

    for q in range(CHUNKS):
        arrived(1 - y, q)

        @pl.when(y == 1)
        def _():
            inward(0, q).start()

        inward(1, q).start()

        @pl.when(is_mid)
        def _():
            send_out(0, q)

    def own(i, carry):
        rows = pl.ds(pl.multiple_of(i * PIECE, PIECE), PIECE)
        at = pl.ds(pl.multiple_of(grp * quarter_rows + i * PIECE, PIECE), PIECE)
        whole[:, at, :] = tgt[:, rows, :]
        return carry

    lax.fori_loop(0, quarter_rows // PIECE, own, 0)

    def target_from(n):
        r = (mate, cross, cross_mate)[n]
        remote(
            tgt, whole.at[:, quarter(r)], t_send.at[n], t_recv.at[n], to_mate
        ).wait_recv()

    target_from(1)
    target_to(2).start()
    target_from(0)
    target_from(2)

    half_planes = NG // 2
    per_chunk = half_planes // CHUNKS

    def forward_own(k):
        def body(i, carry):
            forward(k, y * half_planes + i * FPLANES)
            return carry

        lax.fori_loop(0, half_planes // FPLANES, body, 0)

    def forward_other(k):
        ready = FPLANES // per_chunk

        def body(i, carry):
            for j in range(ready):
                q = i * ready + j
                remote(
                    give.at[k, part(q)], pool.at[k, part(q, (1 - y) * half_rows)],
                    give_sem.at[k, q], pool_sem.at[k, q], to_buddy,
                ).wait_recv()
            forward(k, (1 - y) * half_planes + i * FPLANES)
            return carry

        lax.fori_loop(0, half_planes // FPLANES, body, 0)

    def near_from(n, i):
        remote(
            over.at[share(0, i)], near.at[n, share(0, i)],
            near_send.at[n, i], near_recv.at[n, i], to_mate,
        ).wait_recv()

    def back(k):
        def body(turn, carry):
            backward(k, jnp.where(turn == 0, 1 - x, x) * BPLANES)

            @pl.when(k == STOPS - 1)
            def _():
                for i in range(2):
                    sum_to_mate(turn, i).start()

                @pl.when(turn == 0)
                def _():
                    for i in range(2):
                        near_from(0, i)
                        across[share(0, i), :] = total[share(cross, i), :] + near[0, share(0, i), :]
                        sum_to_cross(i).start()

            return carry

        lax.fori_loop(0, 2, body, 0)

    def step(t, carry):
        def comm(q):
            @pl.when(is_end & (t < SLOTS))
            def _():
                arrived(2 + t, q)

            @pl.when(is_mid & (t < SLOTS - 1))
            def _():
                arrived(jnp.where(t == 0, 3, t + 4), q)

                @pl.when(t < 2)
                def _():
                    arrived(2 + 2 * t, q)
                    inward(t + 2, q).start()

                send_out(t + 1, q)

            @pl.when((t >= 1) & (t < SLOTS))
            def _():
                choose(t - 1, q)

        comm(0)

        @pl.when(t == 0)
        def _():
            lax.fori_loop(0, NG // PREP, prepare, 0)

        @pl.when(t >= 2)
        def _():
            forward_other(t - 2)

        comm(1)

        @pl.when(t >= 2)
        def _():
            lax.fori_loop(0, NG // MROWS, middle, 0)

        comm(2)

        @pl.when(t >= 2)
        def _():
            back(t - 2)

        comm(3)

        @pl.when((t >= 1) & (t < SLOTS))
        def _():
            forward_own(t - 1)

        return carry

    lax.fori_loop(0, STOPS + 2, step, 0)

    for i in range(2):
        near_from(1, i)
        remote(
            across.at[share(0, i)], over.at[share(0, i)],
            x_send.at[i], x_recv.at[i], to_cross,
        ).wait_recv()
        part_planes = BPLANES // 4
        for j in range(i * part_planes, (i + 1) * part_planes):
            v = total[rows_of(grp * 2 * part_planes + j), :] + near[1, rows_of(j), :] + over[rows_of(j), :]
            a, b = interleave(v[:HALF], v[HALF:])
            out[0, lines_of(j), :] = a
            out[1, lines_of(j), :] = b

    for n in range(3):
        target_to(n).wait_send()
    for i in range(2):
        sum_to_cross(i).wait_send()
        for n in range(2):
            sum_to_mate(n, i).wait_send()

    def drain(q, carry):
        swap(q).wait_send()
        for k in range(STOPS):
            handing(k, q).wait_send()
        for s in range(2):
            inward(s, q).wait_send()

        @pl.when(is_mid)
        def _():
            for s in range(2, 4):
                inward(s, q).wait_send()
            for s in range(SLOTS):
                outward(s, q).wait_send()

        return carry

    lax.fori_loop(0, CHUNKS, drain, 0)


def plane_exchange(offsets, scaled, quarter, consts):
    along_x, along_y, back_y, z_high, z_low, plane, wave = consts
    z_high, z_low = z_high[:LANES, :LANES], z_low[:LANES, :LANES]
    z_table = jnp.block([[z_high, z_low], [z_high, jnp.zeros_like(z_low)]])
    mats = [along_x, along_y, back_y, z_table, plane]
    rows = scaled.shape[0]
    half = rows // 2
    targets, part = quarter.shape[:2]
    smem = pl.BlockSpec(memory_space=pltpu.SMEM)
    vmem = pl.BlockSpec(memory_space=pltpu.VMEM)
    dma = pltpu.SemaphoreType.DMA
    box = functools.partial(pltpu.VMEM, dtype=jnp.float32)
    return pl.pallas_call(
        exchange_kernel,
        out_shape=jax.ShapeDtypeStruct(quarter.shape, jnp.float32),
        in_specs=[smem, smem] + [vmem] * (2 + len(mats)),
        out_specs=vmem,
        scratch_shapes=[
            box((8, half, LANES)),
            box((SLOTS, half, LANES)),
            box((STOPS, half, LANES)),
            box((STOPS, rows, LANES)),
            box((targets, rows, LANES)),
            box((NG * NG, LANES)),
            box((NG * NG, LANES)),
            box((NG * NG, LANES)),
            box((NG * NG, LANES)),
            box((NG * PITCH, LANES)),
            box((2, targets * part, LANES)),
            box((targets * part, LANES)),
            box((targets * part, LANES)),
            dma((8, CHUNKS)),
            dma((CHUNKS,)),
            dma((4, CHUNKS)),
            dma((SLOTS, CHUNKS)),
            dma((STOPS, CHUNKS)),
            dma((STOPS, CHUNKS)),
            dma((3,)),
            dma((3,)),
            dma((2, 2)),
            dma((2, 2)),
            dma((2,)),
            dma((2,)),
        ],
        compiler_params=pltpu.CompilerParams(
            vmem_limit_bytes=48 * 1024 * 1024, collective_id=0, has_side_effects=True
        ),
        cost_estimate=pl.CostEstimate(
            flops=40_000_000_000, bytes_accessed=8_000_000, transcendentals=0
        ),
    )(offsets, wave, scaled, quarter, *mats)


def ring_order(count):
    return list(range(0, count, 2)) + list(range(1, count, 2))[::-1]


def arrival(count):
    order = ring_order(count)
    place = [order.index(i) for i in range(count)]
    worst = [0] * STOPS
    for b in range(count):
        for off in range(count):
            steps = []
            for k in range(STOPS):
                d = (place[b] - place[(b - off - k) % count]) % count
                steps.append(min(d, count - d))
            worst = [max(w, s) for w, s in zip(worst, sorted(steps))]
    return worst


def partner(value, axis, bit):
    return lax.ppermute(value, axis, [(i, i ^ bit) for i in range(lax.axis_size(axis))])


def gather_rows(quarter, axis):
    me = lax.axis_index(axis)
    count = lax.axis_size(axis)
    parts = {0: quarter}
    bit = count // 2
    while bit:
        for key, value in list(parts.items()):
            parts[key ^ bit] = partner(value, axis, bit)
        bit //= 2
    ordered = []
    keys = sorted(parts)
    level = [parts[k] for k in keys]
    bit = 1
    while bit < count:
        swap = (me // bit) % 2 == 1
        merged = []
        for i in range(0, len(level), 2):
            a, b = level[i], level[i + 1]
            merged.append(
                jnp.concatenate([jnp.where(swap, b, a), jnp.where(swap, a, b)], axis=1)
            )
        level = merged
        bit *= 2
    return level[0]


def scatter_rows(total, axis):
    me = lax.axis_index(axis)
    count = lax.axis_size(axis)
    targets, rows, lanes = total.shape
    value = total.reshape((targets, count, rows // count, lanes))
    bit = 1
    while bit < count:
        mine = (me // bit) % 2 == 1
        pairs = value.reshape((targets, value.shape[1] // 2, 2) + value.shape[2:])
        low, high = pairs[:, :, 0], pairs[:, :, 1]
        value = jnp.where(mine, high, low) + partner(jnp.where(mine, low, high), axis, bit)
        bit *= 2
    return value[:, 0]


def local(targets, sources, occupation, offsets):
    count = lax.axis_size("blk")
    target_count, cells = targets.shape[0], sources.shape[1]
    consts = [jnp.asarray(v) for v in tables()]
    scaled = sources * jnp.sqrt(occupation.astype(jnp.float32) * 0.5)[:, None]
    scaled = scaled.reshape(cells // LANES, LANES)
    quarter = targets.reshape(target_count, targets.shape[1] // LANES, LANES)
    if count == 2 * STOPS and lax.axis_size("grp") == 4:
        return plane_exchange(offsets, scaled, quarter, consts).reshape(targets.shape)
    whole = gather_rows(quarter, "grp")

    order = ring_order(count)
    up = [(order[i], order[(i + 1) % count]) for i in range(count)]
    down = [(b, a) for a, b in up]
    worst = arrival(count)
    pool = [scaled]
    ahead = behind = scaled
    for step in range(1, count // 2 + 1):
        if step < count // 2:
            ahead = lax.ppermute(ahead, "blk", up)
            behind = lax.ppermute(behind, "blk", down)
            pool += [ahead, behind]
        else:
            half = scaled.shape[0] // 2
            upper = lax.ppermute(ahead[:half], "blk", up)
            lower = lax.ppermute(behind[half:], "blk", down)
            pool += [jnp.concatenate([upper, lower], axis=0)]

    place = np.zeros(count, np.int32)
    place[order] = np.arange(count)
    place = jnp.asarray(place)
    me = lax.axis_index("blk")
    offset = lax.dynamic_index_in_dim(offsets, lax.axis_index("grp"), 0, keepdims=False)
    block = (me - offset - jnp.arange(STOPS, dtype=jnp.int32)) % count
    back = (place[me] - place[block]) % count
    slot = jnp.where(
        back == 0, 0, jnp.where(back <= count // 2, 2 * back - 1, 2 * (count - back))
    ).astype(jnp.int32)
    rank = jnp.sum((slot[None, :] < slot[:, None]).astype(jnp.int32), axis=1)
    ranked = jnp.sum(
        jnp.where(rank[None, :] == jnp.arange(STOPS)[:, None], slot[None, :], 0), axis=1
    ).astype(jnp.int32)

    total = None
    for first, end in CALLS:
        there = pool[: 2 * worst[end - 1] + 1]
        total = exchange_terms(ranked[first:end], there, whole, total, consts)
    return scatter_rows(total, "grp").reshape(targets.shape)


def solution(mesh):
    in_specs = (P("blk", "grp"), P(("grp", "blk"), None), P(("grp", "blk")), P())
    out_specs = P("blk", "grp")
    return jax.shard_map(local, mesh=mesh, in_specs=in_specs, out_specs=out_specs, check_vma=False)
```

```python
import functools
import math

import jax
import jax.numpy as jnp
import numpy as np
from jax import lax
from jax.experimental import pallas as pl
from jax.experimental.pallas import tpu as pltpu
from jax.sharding import PartitionSpec as P

NG = 64
STOPS = 4
LANES = 128

box_length = 16.0
screen_square = 0.25


def split_np(table):
    high = table.astype(jnp.bfloat16)
    low = (table - high.astype(np.float64)).astype(jnp.bfloat16)
    return high, low


def stacked(table):
    high, low = split_np(table)
    return np.concatenate(
        [np.concatenate([high, high], axis=1), np.concatenate([low, low], axis=1)], axis=0
    )


def tables():
    counter = np.arange(NG)
    angle = 2.0 * np.pi * (counter[:, None] * counter[None, :] % NG) / NG
    cas = (np.cos(angle) + np.sin(angle)) / math.sqrt(NG)
    order = np.concatenate([counter[0::2], counter[1::2]])
    along_x = stacked(cas)
    along_y = stacked(cas[:, order])
    back_y = stacked(cas[order, :])
    z_high, z_low = split_np(np.kron(np.eye(4), cas))
    freq = np.where(counter < NG // 2, counter, counter - NG)
    wave = (2.0 * np.pi * freq / box_length) ** 2
    plane = wave[:, None] + np.tile(wave, 2)[None, :] + screen_square
    return along_x, along_y, back_y, z_high, z_low, plane.astype(np.float32), wave.astype(np.float32)


def split(value):
    high = value.astype(jnp.bfloat16)
    low = (value - high.astype(jnp.float32)).astype(jnp.bfloat16)
    return high, low


def left(table, value):
    high, low = split(value)
    both = jnp.dot(
        table, jnp.concatenate([high, low], axis=0), preferred_element_type=jnp.float32
    )
    return both[:NG] + both[NG:]


def right(z_high, z_low, value):
    high, low = split(value)
    dot = functools.partial(jnp.dot, preferred_element_type=jnp.float32)
    return dot(high, z_high) + (dot(low, z_high) + dot(high, z_low))


HALF = NG // 2
XB = 16
YB = 8
CALLS = ((0, 1), (1, 3), (3, 4))


def pair_kernel(count, has_prior, slots, wave, *refs):
    pool = refs[:count]
    refs = refs[count:]
    targets, along_x, along_y, back_y, z_high, z_low, plane = refs[:7]
    refs = refs[7:]
    if has_prior:
        prior, refs = refs[0], refs[1:]
    out, src, field, sems = refs
    ns = src.shape[0]
    xb, yb = XB * 2 // ns, YB * 2 // ns
    width = ns * LANES

    def wide(parts):
        return jnp.concatenate(parts, axis=1) if ns > 1 else parts[0]

    def load(rows):
        return wide([field[s, rows, :] for s in range(ns)])

    def store(rows, v):
        for s in range(ns):
            field[s, rows, :] = v[:, s * LANES : (s + 1) * LANES]

    for s in range(ns):
        for i in range(count):
            @pl.when(slots[s] == i)
            def _():
                pltpu.make_async_copy(pool[i], src.at[s], sems.at[s]).start()
    for s in range(ns):
        pltpu.make_async_copy(pool[0], src.at[s], sems.at[s]).wait()

    first = lax.broadcasted_iota(jnp.int32, (HALF, LANES), 1) < NG

    def interleave(a, b):
        even = jnp.where(first, a, pltpu.roll(b, NG, 1))
        odd = jnp.where(first, pltpu.roll(a, NG, 1), b)
        return even, odd

    def source_rows(s, x):
        v = src[s, pl.ds(pl.multiple_of(x * HALF, HALF), HALF), :]
        even, odd = interleave(v, v)
        return jnp.concatenate([even, odd], axis=0)

    def source_plane(x):
        return wide([source_rows(s, x) for s in range(ns)])

    def forward(step, carry):
        slabs = []
        for k in range(xb):
            x = step * xb + k
            rows = pl.ds(pl.multiple_of(x * HALF, HALF), HALF)
            even, odd = interleave(targets[0, rows, :], targets[1, rows, :])
            t = jnp.concatenate([even, odd], axis=0)
            slabs.append(wide([t] * ns) * source_plane(x))
        lines = right(z_high[:width, :width], z_low[:width, :width], jnp.concatenate(slabs, axis=0))
        for k in range(xb):
            x = step * xb + k
            rows = pl.ds(pl.multiple_of(x * NG, NG), NG)
            store(rows, left(along_y[...], lines[k * NG : (k + 1) * NG]))
        return carry

    def middle(step, carry):
        group = [step * yb + k for k in range(yb)]
        slabs = []
        for y in group:
            rows = pl.ds(y, NG, stride=PITCH)
            slabs.append(load(rows))
        slabs = [left(along_x[...], v) for v in slabs]
        for k, y in enumerate(group):
            factor = (4.0 * math.pi) / (plane[...] + wave[y])
            slabs[k] = slabs[k] * wide([factor] * ns)
        slabs = [left(along_x[...], v) for v in slabs]
        for y, v in zip(group, slabs):
            rows = pl.ds(y, NG, stride=PITCH)
            store(rows, v)
        return carry

    def backward(step, carry):
        slabs = []
        for k in range(xb):
            x = step * xb + k
            rows = pl.ds(pl.multiple_of(x * NG, NG), NG)
            slabs.append(left(back_y[...], load(rows)))
        lines = right(z_high[:width, :width], z_low[:width, :width], jnp.concatenate(slabs, axis=0))
        for k in range(xb):
            x = step * xb + k
            v = lines[k * NG : (k + 1) * NG] * source_plane(x)
            v = sum(v[:, s * LANES : (s + 1) * LANES] for s in range(ns))
            a, b = interleave(v[:HALF], v[HALF:])
            rows = pl.ds(pl.multiple_of(x * HALF, HALF), HALF)
            if has_prior:
                out[0, rows, :] = prior[0, rows, :] - a
                out[1, rows, :] = prior[1, rows, :] - b
            else:
                out[0, rows, :] = -a
                out[1, rows, :] = -b
        return carry

    lax.fori_loop(0, NG // xb, forward, 0)
    lax.fori_loop(0, NG // yb, middle, 0)
    lax.fori_loop(0, NG // xb, backward, 0)


def exchange_terms(slots, pool, targets, prior, consts):
    *mats, wave = consts
    rows = targets.shape[1]
    ns = slots.shape[0]
    smem = pl.BlockSpec(memory_space=pltpu.SMEM)
    vmem = pl.BlockSpec(memory_space=pltpu.VMEM)
    anywhere = pl.BlockSpec(memory_space=pl.ANY)
    extra = [] if prior is None else [prior]
    return pl.pallas_call(
        functools.partial(pair_kernel, len(pool), prior is not None),
        out_shape=jax.ShapeDtypeStruct(targets.shape, jnp.float32),
        in_specs=[smem, smem] + [anywhere] * len(pool) + [vmem] * (1 + len(mats) + len(extra)),
        out_specs=vmem,
        scratch_shapes=[
            pltpu.VMEM((ns, rows, LANES), jnp.float32),
            pltpu.VMEM((ns, NG * NG, LANES), jnp.float32),
            pltpu.SemaphoreType.DMA((ns,)),
        ],
        compiler_params=pltpu.CompilerParams(vmem_limit_bytes=40 * 1024 * 1024),
        cost_estimate=pl.CostEstimate(
            flops=10_000_000_000 * ns, bytes_accessed=8_000_000, transcendentals=0
        ),
    )(slots, wave, *pool, targets, *mats, *extra)


CHUNKS = 4
SLOTS = 5
PIECE = 64
FPLANES = 32
LATE = 16
BPLANES = 32
MROWS = 32
PITCH = 72
PREP = 4


def exchange_kernel(
    offsets_in, electrons_in, raw, tgt, turns_in, z_table_in, waves_in, out,
    offsets, electrons, turns, z_table, waves,
    src, held, outbox, give, pool, whole, paired, factor, doubled, total, field, near, over, across,
    held_sem, a_sem, inner_sem, outer_sem, give_sem, pool_sem,
    local_sem, t_send, t_recv, near_send, near_recv, x_send, x_recv,
):
    planes = lax.axis_size("blk") // 2
    half_rows = src.shape[0] // 2
    chunk_rows = half_rows // CHUNKS
    quarter_rows = tgt.shape[0]
    me, grp = lax.axis_index("blk"), lax.axis_index("grp")
    z, y = me // 2, me % 2
    buddy = 2 * z + 1 - y
    x, core = grp // 2, grp % 2
    mate = 2 * x + 1 - core
    cross = 2 * (1 - x) + core
    cross_mate = 2 * (1 - x) + 1 - core
    is_end = (z == 0) | (z == planes - 1)
    is_mid = jnp.logical_not(is_end)
    z_in = 1 + z % 2
    z_out = (planes - 1) * jnp.maximum(z - 1, 0)
    z_far = planes - 1 - z_out
    to_buddy, to_in = {"blk": buddy}, {"blk": 2 * z_in + y}
    to_out = {"blk": 2 * z_out + y}
    to_mate, to_cross = {"grp": mate}, {"grp": cross}

    def remote(a, b, send, recv, device):
        return pltpu.make_async_remote_copy(
            src_ref=a, dst_ref=b, send_sem=send, recv_sem=recv,
            device_id=device, device_id_type=pl.DeviceIdType.MESH,
        )

    loads = [
        pltpu.make_async_copy(a, b, local_sem.at[i])
        for i, (a, b) in enumerate(
            (
                (raw, src),
                (electrons_in, electrons),
                (offsets_in, offsets),
                (waves_in, waves),
                (z_table_in, z_table),
                (turns_in, turns),
                (tgt, whole.at[pl.ds(pl.multiple_of(grp * tgt.shape[0], tgt.shape[0]), tgt.shape[0])]),
            )
        )
    ]
    for load in loads:
        load.start()

    barrier = pltpu.get_barrier_semaphore()
    for device in (to_buddy, to_in, to_mate, to_cross):
        pl.semaphore_signal(barrier, inc=1, device_id=device, device_id_type=pl.DeviceIdType.MESH)

    loads[0].wait()
    loads[1].wait()
    scale = jnp.sqrt(jnp.full((PIECE, LANES), electrons[0].astype(jnp.float32) * 0.5))

    def rescale(i, carry):
        rows = pl.ds(pl.multiple_of(i * PIECE, PIECE), PIECE)
        src[rows, :] = src[rows, :] * scale
        return carry

    lax.fori_loop(0, src.shape[0] // PIECE, rescale, 0)

    @pl.when(is_mid)
    def _():
        pl.semaphore_signal(barrier, inc=1, device_id=to_out, device_id_type=pl.DeviceIdType.MESH)
        pl.semaphore_wait(barrier, 5)

    @pl.when(is_end)
    def _():
        pl.semaphore_wait(barrier, 4)

    def part(q, base=0):
        return pl.ds(pl.multiple_of(base + q * chunk_rows, chunk_rows), chunk_rows)

    def swap(q):
        return remote(
            src.at[part(q, (1 - y) * half_rows)], held.at[y, part(q)],
            a_sem.at[q], held_sem.at[y, q], to_buddy,
        )

    def inward(s, q):
        at = jnp.where(s < 2, s, 2 * (s - 1))
        to = jnp.where(is_end, 2 + 2 * s, jnp.where(s == 0, 3, s + 4))
        return remote(
            held.at[at, part(q)], held.at[to, part(q)],
            inner_sem.at[s, q], held_sem.at[to, q], to_in,
        )

    def outward(s, q):
        return remote(
            outbox.at[s, part(q)], held.at[2 + s, part(q)],
            outer_sem.at[s, q], held_sem.at[2 + s, q], to_out,
        )

    def handing(k, q):
        return remote(
            give.at[k, part(q)], pool.at[k, part(q, y * half_rows)],
            give_sem.at[k, q], pool_sem.at[k, q], to_buddy,
        )

    def arrived(p, q):
        remote(
            held.at[p, part(q)], held.at[p, part(q)],
            a_sem.at[q], held_sem.at[p, q], to_buddy,
        ).wait_recv()

    def quarter(r):
        return pl.ds(pl.multiple_of(r * quarter_rows, quarter_rows), quarter_rows)

    def share(r, i):
        n = quarter_rows // 2
        return pl.ds(pl.multiple_of((2 * r + i) * n, n), n)

    def target_to(n):
        if n == 0:
            a, r, device = tgt, grp, to_mate
        elif n == 1:
            a, r, device = tgt, grp, to_cross
        else:
            a, r, device = whole.at[quarter(cross)], cross, to_mate
        return remote(a, whole.at[quarter(r)], t_send.at[n], t_recv.at[n], device)

    def sum_to_mate(n, i):
        r = jnp.where(n == 0, cross_mate, mate)
        return remote(
            total.at[share(r, i)], near.at[n, share(0, i)],
            near_send.at[n, i], near_recv.at[n, i], to_mate,
        )

    def sum_to_cross(i):
        return remote(
            across.at[share(0, i)], over.at[share(0, i)],
            x_send.at[i], x_recv.at[i], to_cross,
        )

    first = lax.broadcasted_iota(jnp.int32, (HALF, LANES), 1) < NG

    def interleave(a, b):
        even = jnp.where(first, a, pltpu.roll(b, NG, 1))
        odd = jnp.where(first, pltpu.roll(a, NG, 1), b)
        return even, odd

    def rows_of(at, n=1):
        return pl.ds(pl.multiple_of(at * NG, NG), n * NG)

    def lines_of(at):
        return pl.ds(pl.multiple_of(at * HALF, HALF), HALF)

    def along_z(value):
        high, low = split(value)
        both = jnp.dot(
            jnp.concatenate([high, low], axis=1), z_table[...], preferred_element_type=jnp.float32
        )
        return both[:, :LANES] + both[:, LANES:]

    def rotate(table, values):
        out = []
        for i in range(0, len(values), 2):
            both = left(table[...], jnp.concatenate(values[i : i + 2], axis=1))
            out += [both[:, :LANES], both[:, LANES:]]
        return out

    def prepare(step, carry):
        for i in range(PREP):
            at = step * PREP + i
            even, odd = interleave(
                whole[pl.ds(at * NG, HALF, stride=2), :], whole[pl.ds(at * NG + 1, HALF, stride=2), :]
            )
            paired[rows_of(at), :] = jnp.concatenate([even, odd], axis=0)
        return carry

    def weigh(step, carry):
        for i in range(PREP):
            at = step * PREP + i
            factor[rows_of(at), :] = (4.0 * math.pi) / (waves[:NG, :] + waves[pl.ds(NG + at, 1), :])
        return carry

    def forward(k, base, count):
        slabs = []
        for i in range(count):
            at = base + i
            v = pool[k, lines_of(at), :]
            even, odd = interleave(v, v)
            v = jnp.concatenate([even, odd], axis=0)
            doubled[rows_of(at), :] = v
            slabs.append(paired[rows_of(at), :] * v)
        lines = along_z(jnp.concatenate(slabs, axis=0))
        slabs = rotate(turns.at[1], [lines[i * NG : (i + 1) * NG] for i in range(count)])
        for i, v in enumerate(slabs):
            field[pl.ds(pl.multiple_of(base * PITCH, 8) + i * PITCH, NG), :] = v

    def middle(step, carry):
        group = [step * MROWS + i for i in range(MROWS)]
        slabs = rotate(turns.at[0], [field[pl.ds(at, NG, stride=PITCH), :] for at in group])
        slabs = [v * factor[rows_of(at), :] for at, v in zip(group, slabs)]
        slabs = rotate(turns.at[0], slabs)
        for at, v in zip(group, slabs):
            field[pl.ds(at, NG, stride=PITCH), :] = v
        return carry

    def backward(k, base, count):
        slabs = rotate(turns.at[2], [
            field[pl.ds(pl.multiple_of(base * PITCH, 8) + i * PITCH, NG), :] for i in range(count)
        ])
        lines = along_z(jnp.concatenate(slabs, axis=0))
        for i in range(count):
            rows = rows_of(base + i)
            v = lines[i * NG : (i + 1) * NG] * doubled[rows, :]
            total[rows, :] = jnp.where(k == 0, 0.0, total[rows, :]) - v

    for q in range(CHUNKS):
        swap(q).start()
    target_to(0).start()
    target_to(1).start()

    def keep(i, carry):
        rows = pl.ds(pl.multiple_of(i * PIECE, PIECE), PIECE)
        at = pl.ds(pl.multiple_of(y * half_rows + i * PIECE, PIECE), PIECE)
        held[y, rows, :] = src[at, :]
        return carry

    lax.fori_loop(0, half_rows // PIECE, keep, 0)

    @pl.when(y == 0)
    def _():
        for q in range(CHUNKS):
            inward(0, q).start()

    loads[2].wait()
    off = offsets[grp]

    def flag(value):
        return value.astype(jnp.int32)

    cycle = 2 * planes

    def needs(b, c):
        return flag(lax.rem(b - c - off + 2 * cycle, cycle) < STOPS)

    end = jnp.where(is_end, z, z_out)
    line = []
    for d in range(1, planes):
        p = jnp.where(end == 0, d, planes - 1 - d)
        line += [2 * p, 2 * p + 1]
    skip = jnp.int32(0)
    found = jnp.int32(0)
    for i, c in enumerate(line):
        spare = (1 - found) * (1 - needs(2 * end, c)) * (1 - needs(2 * end + 1, c))
        skip = skip + i * spare
        found = found + spare
    mid_ids = [2 * z, 2 * z + 1, 2 * z_out, 2 * z_in, 2 * z_out + 1, 2 * z_in + 1, 2 * z_far, 2 * z_far + 1]
    end_ids = [2 * z, 2 * z + 1]
    end_ids += [jnp.where(s < skip, line[s], line[s + 1]) for s in range(SLOTS)]

    def places(b):
        rank = jnp.int32(0)
        at = [jnp.int32(0)] * STOPS
        for p, c in enumerate(mid_ids):
            if p < len(end_ids):
                want = needs(b, jnp.where(is_end, end_ids[p], c))
            else:
                want = jnp.where(is_end, 0, needs(b, c))
            for k in range(STOPS):
                at[k] = at[k] + (p - k) * want * flag(rank == k)
            rank = rank + want
        return at

    my_places, buddy_places = places(me), places(buddy)

    def pick(places, k):
        return sum(jnp.where(k == i, places[i], 0) for i in range(STOPS))

    def send_out(s, q):
        first = jnp.where(s < 2, s, jnp.where(s == 2, 3, s + 2))
        second = jnp.where(s + 1 < 2, s + 1, jnp.where(s + 1 == 2, 3, s + 3))
        for i in range(chunk_rows // PIECE):
            rows = pl.ds(pl.multiple_of(q * chunk_rows + i * PIECE, PIECE), PIECE)
            outbox[s, rows, :] = jnp.where(s < skip, held[first, rows, :], held[second, rows, :])
        outward(s, q).start()

    def choose(k, q):
        mine, other = pick(my_places, k), pick(buddy_places, k)
        short = flag(is_end)
        for i in range(chunk_rows // PIECE):
            rows = pl.ds(pl.multiple_of(q * chunk_rows + i * PIECE, PIECE), PIECE)
            a = b = held[k, rows, :]
            for j in range(1, STOPS + 1):
                at = k + j - (short if j == STOPS else 0)
                v = held[at, rows, :]
                a = jnp.where(mine == j, v, a)
                b = jnp.where(other == j, v, b)
            give[k, rows, :] = b
            at = pl.multiple_of(y * half_rows + q * chunk_rows + i * PIECE, PIECE)
            pool[k, pl.ds(at, PIECE), :] = a
        handing(k, q).start()

    for load in loads[3:]:
        load.wait()
    lax.fori_loop(0, NG // PREP, weigh, 0)

    def open_up(q, carry):
        arrived(1 - y, q)

        @pl.when(y == 1)
        def _():
            inward(0, q).start()

        inward(1, q).start()

        @pl.when(is_mid)
        def _():
            send_out(0, q)

        return carry

    lax.fori_loop(0, CHUNKS, open_up, 0)

    def target_from(n):
        r = (mate, cross, cross_mate)[n]
        remote(
            tgt, whole.at[quarter(r)], t_send.at[n], t_recv.at[n], to_mate
        ).wait_recv()

    half_planes = NG // 2
    per_chunk = half_planes // CHUNKS

    def forward_own(k):
        def body(i, carry):
            forward(k, y * half_planes + i * FPLANES, FPLANES)
            return carry

        lax.fori_loop(0, half_planes // FPLANES, body, 0)

    def forward_other(k):
        ready = LATE // per_chunk

        def body(i, carry):
            for j in range(ready):
                q = i * ready + j
                remote(
                    give.at[k, part(q)], pool.at[k, part(q, (1 - y) * half_rows)],
                    give_sem.at[k, q], pool_sem.at[k, q], to_buddy,
                ).wait_recv()
            forward(k, (1 - y) * half_planes + i * LATE, LATE)
            return carry

        lax.fori_loop(0, half_planes // LATE, body, 0)

    def near_from(n, i):
        remote(
            over.at[share(0, i)], near.at[n, share(0, i)],
            near_send.at[n, i], near_recv.at[n, i], to_mate,
        ).wait_recv()

    share_planes = NG // 8

    def back(k):
        @pl.when(k < STOPS - 1)
        def _():
            def body(i, carry):
                backward(k, i * BPLANES, BPLANES)
                return carry

            lax.fori_loop(0, NG // BPLANES, body, 0)

        @pl.when(k == STOPS - 1)
        def _():
            def away(i, carry):
                backward(k, (2 * cross_mate + i) * share_planes, share_planes)
                sum_to_mate(0, i).start()
                backward(k, (2 * cross + i) * share_planes, share_planes)
                near_from(0, i)
                across[share(0, i), :] = total[share(cross, i), :] + near[0, share(0, i), :]
                sum_to_cross(i).start()
                return carry

            lax.fori_loop(0, 2, away, 0)

            def home(i, carry):
                r = jnp.where(i == 0, mate, grp)
                backward(k, 2 * r * share_planes, 2 * share_planes)

                @pl.when(i == 0)
                def _():
                    for j in range(2):
                        sum_to_mate(1, j).start()

                return carry

            lax.fori_loop(0, 2, home, 0)

    def step(t, carry):
        def chunk(q, carry):
            @pl.when(is_end & (t < SLOTS))
            def _():
                arrived(2 + t, q)

            @pl.when(is_mid & (t < SLOTS - 1))
            def _():
                arrived(jnp.where(t == 0, 3, t + 4), q)

                @pl.when(t < 2)
                def _():
                    arrived(2 + 2 * t, q)
                    inward(t + 2, q).start()

                send_out(t + 1, q)

            @pl.when((t >= 1) & (t < SLOTS))
            def _():
                choose(t - 1, q)

            return carry

        def comm(n):
            lax.fori_loop(n * CHUNKS // 4, (n + 1) * CHUNKS // 4, chunk, 0)

        comm(0)

        @pl.when(t == 0)
        def _():
            target_from(1)
            target_to(2).start()

        @pl.when(t >= 2)
        def _():
            forward_other(t - 2)

        comm(1)

        @pl.when(t >= 2)
        def _():
            lax.fori_loop(0, NG // MROWS, middle, 0)

        comm(2)

        @pl.when(t >= 2)
        def _():
            back(t - 2)

        @pl.when(t == 0)
        def _():
            target_from(0)
            target_from(2)
            lax.fori_loop(0, NG // PREP, prepare, 0)

        comm(3)

        @pl.when((t >= 1) & (t < SLOTS))
        def _():
            forward_own(t - 1)

        return carry

    lax.fori_loop(0, STOPS + 2, step, 0)

    for i in range(2):
        near_from(1, i)
        remote(
            across.at[share(0, i)], over.at[share(0, i)],
            x_send.at[i], x_recv.at[i], to_cross,
        ).wait_recv()
        for j in range(i * share_planes, (i + 1) * share_planes):
            v = total[rows_of(2 * grp * share_planes + j), :] + near[1, rows_of(j), :] + over[rows_of(j), :]
            a, b = interleave(v[:HALF], v[HALF:])
            out[pl.ds(j * NG, HALF, stride=2), :] = a
            out[pl.ds(j * NG + 1, HALF, stride=2), :] = b

    for n in range(3):
        target_to(n).wait_send()
    for i in range(2):
        sum_to_cross(i).wait_send()
        for n in range(2):
            sum_to_mate(n, i).wait_send()

    def drain(q, carry):
        swap(q).wait_send()
        for k in range(STOPS):
            handing(k, q).wait_send()
        for s in range(2):
            inward(s, q).wait_send()

        @pl.when(is_mid)
        def _():
            for s in range(2, 4):
                inward(s, q).wait_send()
            for s in range(SLOTS):
                outward(s, q).wait_send()

        return carry

    lax.fori_loop(0, CHUNKS, drain, 0)


def packed_tables():
    along_x, along_y, back_y, z_high, z_low, plane, wave = tables()
    z_high, z_low = z_high[:LANES, :LANES], z_low[:LANES, :LANES]
    z_table = np.block([[z_high, z_low], [z_high, np.zeros_like(z_low)]])
    waves = np.concatenate([plane, np.tile(wave[:, None], (1, LANES))], axis=0)
    return [jnp.asarray(v) for v in (np.stack([along_x, along_y, back_y]), z_table, waves)]


def plane_exchange(offsets, occupation, source, quarter):
    tables = packed_tables()
    rows = source.shape[0]
    half = rows // 2
    part = quarter.shape[0]
    vmem = pl.BlockSpec(memory_space=pltpu.VMEM)
    dma = pltpu.SemaphoreType.DMA
    box = functools.partial(pltpu.VMEM, dtype=jnp.float32)
    return pl.pallas_call(
        exchange_kernel,
        out_shape=jax.ShapeDtypeStruct(quarter.shape, jnp.float32),
        in_specs=[pl.BlockSpec(memory_space=pl.ANY)] * (4 + len(tables)),
        out_specs=vmem,
        scratch_shapes=[
            pltpu.SMEM(offsets.shape, jnp.int32),
            pltpu.SMEM(occupation.shape, jnp.int32),
            *[pltpu.VMEM(v.shape, v.dtype) for v in tables],
            box((rows, LANES)),
            box((8, half, LANES)),
            box((SLOTS, half, LANES)),
            box((STOPS, half, LANES)),
            box((STOPS, rows, LANES)),
            box((NG * NG, LANES)),
            box((NG * NG, LANES)),
            box((NG * NG, LANES)),
            box((NG * NG, LANES)),
            box((NG * NG, LANES)),
            box((NG * PITCH, LANES)),
            box((2, part, LANES)),
            box((part, LANES)),
            box((part, LANES)),
            dma((8, CHUNKS)),
            dma((CHUNKS,)),
            dma((4, CHUNKS)),
            dma((SLOTS, CHUNKS)),
            dma((STOPS, CHUNKS)),
            dma((STOPS, CHUNKS)),
            dma((7,)),
            dma((3,)),
            dma((3,)),
            dma((2, 2)),
            dma((2, 2)),
            dma((2,)),
            dma((2,)),
        ],
        compiler_params=pltpu.CompilerParams(
            vmem_limit_bytes=56 * 1024 * 1024, collective_id=0, has_side_effects=True
        ),
        cost_estimate=pl.CostEstimate(
            flops=40_000_000_000, bytes_accessed=8_000_000, transcendentals=0
        ),
    )(offsets, occupation, source, quarter, *tables)


def ring_order(count):
    return list(range(0, count, 2)) + list(range(1, count, 2))[::-1]


def arrival(count):
    order = ring_order(count)
    place = [order.index(i) for i in range(count)]
    worst = [0] * STOPS
    for b in range(count):
        for off in range(count):
            steps = []
            for k in range(STOPS):
                d = (place[b] - place[(b - off - k) % count]) % count
                steps.append(min(d, count - d))
            worst = [max(w, s) for w, s in zip(worst, sorted(steps))]
    return worst


def partner(value, axis, bit):
    return lax.ppermute(value, axis, [(i, i ^ bit) for i in range(lax.axis_size(axis))])


def gather_rows(quarter, axis):
    me = lax.axis_index(axis)
    count = lax.axis_size(axis)
    parts = {0: quarter}
    bit = count // 2
    while bit:
        for key, value in list(parts.items()):
            parts[key ^ bit] = partner(value, axis, bit)
        bit //= 2
    ordered = []
    keys = sorted(parts)
    level = [parts[k] for k in keys]
    bit = 1
    while bit < count:
        swap = (me // bit) % 2 == 1
        merged = []
        for i in range(0, len(level), 2):
            a, b = level[i], level[i + 1]
            merged.append(
                jnp.concatenate([jnp.where(swap, b, a), jnp.where(swap, a, b)], axis=1)
            )
        level = merged
        bit *= 2
    return level[0]


def scatter_rows(total, axis):
    me = lax.axis_index(axis)
    count = lax.axis_size(axis)
    targets, rows, lanes = total.shape
    value = total.reshape((targets, count, rows // count, lanes))
    bit = 1
    while bit < count:
        mine = (me // bit) % 2 == 1
        pairs = value.reshape((targets, value.shape[1] // 2, 2) + value.shape[2:])
        low, high = pairs[:, :, 0], pairs[:, :, 1]
        value = jnp.where(mine, high, low) + partner(jnp.where(mine, low, high), axis, bit)
        bit *= 2
    return value[:, 0]


def local(targets, sources, occupation, offsets):
    count = lax.axis_size("blk")
    target_count, cells = targets.shape[0], sources.shape[1]
    quarter = targets.reshape(target_count, targets.shape[1] // LANES, LANES)
    if count == 2 * STOPS and lax.axis_size("grp") == 4:
        mixed = quarter.transpose(1, 0, 2).reshape(-1, LANES)
        result = plane_exchange(offsets, occupation, sources.reshape(-1, LANES), mixed)
        return result.reshape(-1, target_count, LANES).transpose(1, 0, 2).reshape(targets.shape)
    consts = [jnp.asarray(v) for v in tables()]
    scale = jnp.sqrt(occupation.astype(jnp.float32) * 0.5)
    scaled = (sources * scale[:, None]).reshape(cells // LANES, LANES)
    whole = gather_rows(quarter, "grp")

    order = ring_order(count)
    up = [(order[i], order[(i + 1) % count]) for i in range(count)]
    down = [(b, a) for a, b in up]
    worst = arrival(count)
    pool = [scaled]
    ahead = behind = scaled
    for step in range(1, count // 2 + 1):
        if step < count // 2:
            ahead = lax.ppermute(ahead, "blk", up)
            behind = lax.ppermute(behind, "blk", down)
            pool += [ahead, behind]
        else:
            half = scaled.shape[0] // 2
            upper = lax.ppermute(ahead[:half], "blk", up)
            lower = lax.ppermute(behind[half:], "blk", down)
            pool += [jnp.concatenate([upper, lower], axis=0)]

    place = np.zeros(count, np.int32)
    place[order] = np.arange(count)
    place = jnp.asarray(place)
    me = lax.axis_index("blk")
    offset = lax.dynamic_index_in_dim(offsets, lax.axis_index("grp"), 0, keepdims=False)
    block = (me - offset - jnp.arange(STOPS, dtype=jnp.int32)) % count
    back = (place[me] - place[block]) % count
    slot = jnp.where(
        back == 0, 0, jnp.where(back <= count // 2, 2 * back - 1, 2 * (count - back))
    ).astype(jnp.int32)
    rank = jnp.sum((slot[None, :] < slot[:, None]).astype(jnp.int32), axis=1)
    ranked = jnp.sum(
        jnp.where(rank[None, :] == jnp.arange(STOPS)[:, None], slot[None, :], 0), axis=1
    ).astype(jnp.int32)

    total = None
    for first, end in CALLS:
        there = pool[: 2 * worst[end - 1] + 1]
        total = exchange_terms(ranked[first:end], there, whole, total, consts)
    return scatter_rows(total, "grp").reshape(targets.shape)


def solution(mesh):
    in_specs = (P("blk", "grp"), P(("grp", "blk"), None), P(("grp", "blk")), P())
    out_specs = P("blk", "grp")
    return jax.shard_map(local, mesh=mesh, in_specs=in_specs, out_specs=out_specs, check_vma=False)
```

```python
import functools
import math

import jax
import jax.numpy as jnp
import numpy as np
from jax import lax
from jax.experimental import pallas as pl
from jax.experimental.pallas import tpu as pltpu
from jax.sharding import PartitionSpec as P

NG = 64
STOPS = 4
LANES = 128

box_length = 16.0
screen_square = 0.25


def split_np(table):
    high = table.astype(jnp.bfloat16)
    low = (table - high.astype(np.float64)).astype(jnp.bfloat16)
    return high, low


def stacked(table):
    high, low = split_np(table)
    return np.concatenate(
        [np.concatenate([high, high], axis=1), np.concatenate([low, low], axis=1)], axis=0
    )


def tables():
    counter = np.arange(NG)
    angle = 2.0 * np.pi * (counter[:, None] * counter[None, :] % NG) / NG
    cas = (np.cos(angle) + np.sin(angle)) / math.sqrt(NG)
    order = np.concatenate([counter[0::2], counter[1::2]])
    along_x = stacked(cas)
    along_y = stacked(cas[:, order])
    back_y = stacked(cas[order, :])
    z_high, z_low = split_np(np.kron(np.eye(4), cas))
    freq = np.where(counter < NG // 2, counter, counter - NG)
    wave = (2.0 * np.pi * freq / box_length) ** 2
    plane = wave[:, None] + np.tile(wave, 2)[None, :] + screen_square
    return along_x, along_y, back_y, z_high, z_low, plane.astype(np.float32), wave.astype(np.float32)


def split(value):
    high = value.astype(jnp.bfloat16)
    low = (value - high.astype(jnp.float32)).astype(jnp.bfloat16)
    return high, low


def left(table, value):
    high, low = split(value)
    both = jnp.dot(
        table, jnp.concatenate([high, low], axis=0), preferred_element_type=jnp.float32
    )
    return both[:NG] + both[NG:]


def right(z_high, z_low, value):
    high, low = split(value)
    dot = functools.partial(jnp.dot, preferred_element_type=jnp.float32)
    return dot(high, z_high) + (dot(low, z_high) + dot(high, z_low))


HALF = NG // 2
XB = 16
YB = 8
CALLS = ((0, 1), (1, 3), (3, 4))


def pair_kernel(count, has_prior, slots, wave, *refs):
    pool = refs[:count]
    refs = refs[count:]
    targets, along_x, along_y, back_y, z_high, z_low, plane = refs[:7]
    refs = refs[7:]
    if has_prior:
        prior, refs = refs[0], refs[1:]
    out, src, field, sems = refs
    ns = src.shape[0]
    xb, yb = XB * 2 // ns, YB * 2 // ns
    width = ns * LANES

    def wide(parts):
        return jnp.concatenate(parts, axis=1) if ns > 1 else parts[0]

    def load(rows):
        return wide([field[s, rows, :] for s in range(ns)])

    def store(rows, v):
        for s in range(ns):
            field[s, rows, :] = v[:, s * LANES : (s + 1) * LANES]

    for s in range(ns):
        for i in range(count):
            @pl.when(slots[s] == i)
            def _():
                pltpu.make_async_copy(pool[i], src.at[s], sems.at[s]).start()
    for s in range(ns):
        pltpu.make_async_copy(pool[0], src.at[s], sems.at[s]).wait()

    first = lax.broadcasted_iota(jnp.int32, (HALF, LANES), 1) < NG

    def interleave(a, b):
        even = jnp.where(first, a, pltpu.roll(b, NG, 1))
        odd = jnp.where(first, pltpu.roll(a, NG, 1), b)
        return even, odd

    def source_rows(s, x):
        v = src[s, pl.ds(pl.multiple_of(x * HALF, HALF), HALF), :]
        even, odd = interleave(v, v)
        return jnp.concatenate([even, odd], axis=0)

    def source_plane(x):
        return wide([source_rows(s, x) for s in range(ns)])

    def forward(step, carry):
        slabs = []
        for k in range(xb):
            x = step * xb + k
            rows = pl.ds(pl.multiple_of(x * HALF, HALF), HALF)
            even, odd = interleave(targets[0, rows, :], targets[1, rows, :])
            t = jnp.concatenate([even, odd], axis=0)
            slabs.append(wide([t] * ns) * source_plane(x))
        lines = right(z_high[:width, :width], z_low[:width, :width], jnp.concatenate(slabs, axis=0))
        for k in range(xb):
            x = step * xb + k
            rows = pl.ds(pl.multiple_of(x * NG, NG), NG)
            store(rows, left(along_y[...], lines[k * NG : (k + 1) * NG]))
        return carry

    def middle(step, carry):
        group = [step * yb + k for k in range(yb)]
        slabs = []
        for y in group:
            rows = pl.ds(y, NG, stride=PITCH)
            slabs.append(load(rows))
        slabs = [left(along_x[...], v) for v in slabs]
        for k, y in enumerate(group):
            factor = (4.0 * math.pi) / (plane[...] + wave[y])
            slabs[k] = slabs[k] * wide([factor] * ns)
        slabs = [left(along_x[...], v) for v in slabs]
        for y, v in zip(group, slabs):
            rows = pl.ds(y, NG, stride=PITCH)
            store(rows, v)
        return carry

    def backward(step, carry):
        slabs = []
        for k in range(xb):
            x = step * xb + k
            rows = pl.ds(pl.multiple_of(x * NG, NG), NG)
            slabs.append(left(back_y[...], load(rows)))
        lines = right(z_high[:width, :width], z_low[:width, :width], jnp.concatenate(slabs, axis=0))
        for k in range(xb):
            x = step * xb + k
            v = lines[k * NG : (k + 1) * NG] * source_plane(x)
            v = sum(v[:, s * LANES : (s + 1) * LANES] for s in range(ns))
            a, b = interleave(v[:HALF], v[HALF:])
            rows = pl.ds(pl.multiple_of(x * HALF, HALF), HALF)
            if has_prior:
                out[0, rows, :] = prior[0, rows, :] - a
                out[1, rows, :] = prior[1, rows, :] - b
            else:
                out[0, rows, :] = -a
                out[1, rows, :] = -b
        return carry

    lax.fori_loop(0, NG // xb, forward, 0)
    lax.fori_loop(0, NG // yb, middle, 0)
    lax.fori_loop(0, NG // xb, backward, 0)


def exchange_terms(slots, pool, targets, prior, consts):
    *mats, wave = consts
    rows = targets.shape[1]
    ns = slots.shape[0]
    smem = pl.BlockSpec(memory_space=pltpu.SMEM)
    vmem = pl.BlockSpec(memory_space=pltpu.VMEM)
    anywhere = pl.BlockSpec(memory_space=pl.ANY)
    extra = [] if prior is None else [prior]
    return pl.pallas_call(
        functools.partial(pair_kernel, len(pool), prior is not None),
        out_shape=jax.ShapeDtypeStruct(targets.shape, jnp.float32),
        in_specs=[smem, smem] + [anywhere] * len(pool) + [vmem] * (1 + len(mats) + len(extra)),
        out_specs=vmem,
        scratch_shapes=[
            pltpu.VMEM((ns, rows, LANES), jnp.float32),
            pltpu.VMEM((ns, NG * NG, LANES), jnp.float32),
            pltpu.SemaphoreType.DMA((ns,)),
        ],
        compiler_params=pltpu.CompilerParams(vmem_limit_bytes=40 * 1024 * 1024),
        cost_estimate=pl.CostEstimate(
            flops=10_000_000_000 * ns, bytes_accessed=8_000_000, transcendentals=0
        ),
    )(slots, wave, *pool, targets, *mats, *extra)


CHUNKS = 8
SLOTS = 5
PIECE = 64
FPLANES = 32
LATE = 16
BPLANES = 32
MROWS = 32
PITCH = 72
PREP = 4


def exchange_kernel(
    offsets_in, electrons_in, raw, tgt, turns_in, z_table_in, waves_in, out,
    offsets, electrons, turns, z_table, waves,
    src, held, outbox, give, pool, whole, paired, factor, doubled, total, field, near, over, across,
    held_sem, a_sem, inner_sem, outer_sem, give_sem, pool_sem,
    local_sem, t_send, t_recv, near_send, near_recv, x_send, x_recv,
):
    planes = lax.axis_size("blk") // 2
    half_rows = src.shape[0] // 2
    chunk_rows = half_rows // CHUNKS
    quarter_rows = tgt.shape[0]
    me, grp = lax.axis_index("blk"), lax.axis_index("grp")
    z, y = me // 2, me % 2
    buddy = 2 * z + 1 - y
    x, core = grp // 2, grp % 2
    mate = 2 * x + 1 - core
    cross = 2 * (1 - x) + core
    cross_mate = 2 * (1 - x) + 1 - core
    is_end = (z == 0) | (z == planes - 1)
    is_mid = jnp.logical_not(is_end)
    z_in = 1 + z % 2
    z_out = (planes - 1) * jnp.maximum(z - 1, 0)
    z_far = planes - 1 - z_out
    to_buddy, to_in = {"blk": buddy}, {"blk": 2 * z_in + y}
    to_out = {"blk": 2 * z_out + y}
    to_mate, to_cross = {"grp": mate}, {"grp": cross}

    def remote(a, b, send, recv, device):
        return pltpu.make_async_remote_copy(
            src_ref=a, dst_ref=b, send_sem=send, recv_sem=recv,
            device_id=device, device_id_type=pl.DeviceIdType.MESH,
        )

    loads = [
        pltpu.make_async_copy(a, b, local_sem.at[i])
        for i, (a, b) in enumerate(
            (
                (raw, src),
                (electrons_in, electrons),
                (offsets_in, offsets),
                (waves_in, waves),
                (z_table_in, z_table),
                (turns_in, turns),
                (tgt, whole.at[pl.ds(pl.multiple_of(grp * tgt.shape[0], tgt.shape[0]), tgt.shape[0])]),
            )
        )
    ]
    for load in loads:
        load.start()

    barrier = pltpu.get_barrier_semaphore()
    for device in (to_buddy, to_in, to_mate, to_cross):
        pl.semaphore_signal(barrier, inc=1, device_id=device, device_id_type=pl.DeviceIdType.MESH)

    loads[0].wait()
    loads[1].wait()
    scale = jnp.sqrt(jnp.full((PIECE, LANES), electrons[0].astype(jnp.float32) * 0.5))

    def rescale(i, carry):
        rows = pl.ds(pl.multiple_of(i * PIECE, PIECE), PIECE)
        src[rows, :] = src[rows, :] * scale
        return carry

    lax.fori_loop(0, src.shape[0] // PIECE, rescale, 0)

    @pl.when(is_mid)
    def _():
        pl.semaphore_signal(barrier, inc=1, device_id=to_out, device_id_type=pl.DeviceIdType.MESH)
        pl.semaphore_wait(barrier, 5)

    @pl.when(is_end)
    def _():
        pl.semaphore_wait(barrier, 4)

    def part(q, base=0):
        return pl.ds(pl.multiple_of(base + q * chunk_rows, chunk_rows), chunk_rows)

    def swap(q):
        return remote(
            src.at[part(q, (1 - y) * half_rows)], held.at[y, part(q)],
            a_sem.at[q], held_sem.at[y, q], to_buddy,
        )

    def inward(s, q):
        at = jnp.where(s < 2, s, 2 * (s - 1))
        to = jnp.where(is_end, 2 + 2 * s, jnp.where(s == 0, 3, s + 4))
        return remote(
            held.at[at, part(q)], held.at[to, part(q)],
            inner_sem.at[s, q], held_sem.at[to, q], to_in,
        )

    def outward(s, q):
        return remote(
            outbox.at[s, part(q)], held.at[2 + s, part(q)],
            outer_sem.at[s, q], held_sem.at[2 + s, q], to_out,
        )

    def handing(k, q):
        return remote(
            give.at[k, part(q)], pool.at[k, part(q, y * half_rows)],
            give_sem.at[k, q], pool_sem.at[k, q], to_buddy,
        )

    def arrived(p, q):
        remote(
            held.at[p, part(q)], held.at[p, part(q)],
            a_sem.at[q], held_sem.at[p, q], to_buddy,
        ).wait_recv()

    def quarter(r):
        return pl.ds(pl.multiple_of(r * quarter_rows, quarter_rows), quarter_rows)

    def share(r, i):
        n = quarter_rows // 2
        return pl.ds(pl.multiple_of((2 * r + i) * n, n), n)

    def target_to(n):
        if n == 0:
            a, r, device = tgt, grp, to_mate
        elif n == 1:
            a, r, device = tgt, grp, to_cross
        else:
            a, r, device = whole.at[quarter(cross)], cross, to_mate
        return remote(a, whole.at[quarter(r)], t_send.at[n], t_recv.at[n], device)

    def sum_to_mate(n, i):
        r = jnp.where(n == 0, cross_mate, mate)
        return remote(
            total.at[share(r, i)], near.at[n, share(0, i)],
            near_send.at[n, i], near_recv.at[n, i], to_mate,
        )

    def sum_to_cross(i):
        return remote(
            across.at[share(0, i)], over.at[share(0, i)],
            x_send.at[i], x_recv.at[i], to_cross,
        )

    first = lax.broadcasted_iota(jnp.int32, (HALF, LANES), 1) < NG

    def interleave(a, b):
        even = jnp.where(first, a, pltpu.roll(b, NG, 1))
        odd = jnp.where(first, pltpu.roll(a, NG, 1), b)
        return even, odd

    def rows_of(at, n=1):
        return pl.ds(pl.multiple_of(at * NG, NG), n * NG)

    def lines_of(at):
        return pl.ds(pl.multiple_of(at * HALF, HALF), HALF)

    def along_z(value):
        high, low = split(value)
        both = jnp.dot(
            jnp.concatenate([high, low], axis=1), z_table[...], preferred_element_type=jnp.float32
        )
        return both[:, :LANES] + both[:, LANES:]

    def rotate(table, values):
        out = []
        for i in range(0, len(values), 2):
            both = left(table[...], jnp.concatenate(values[i : i + 2], axis=1))
            out += [both[:, :LANES], both[:, LANES:]]
        return out

    def prepare(step, carry):
        for i in range(PREP):
            at = step * PREP + i
            even, odd = interleave(
                whole[pl.ds(at * NG, HALF, stride=2), :], whole[pl.ds(at * NG + 1, HALF, stride=2), :]
            )
            paired[rows_of(at), :] = jnp.concatenate([even, odd], axis=0)
        return carry

    def weigh(step, carry):
        for i in range(PREP):
            at = step * PREP + i
            factor[rows_of(at), :] = (4.0 * math.pi) / (waves[:NG, :] + waves[pl.ds(NG + at, 1), :])
        return carry

    def forward(k, base, count):
        slabs = []
        for i in range(count):
            at = base + i
            v = pool[k, lines_of(at), :]
            even, odd = interleave(v, v)
            v = jnp.concatenate([even, odd], axis=0)
            doubled[rows_of(at), :] = v
            slabs.append(paired[rows_of(at), :] * v)
        lines = along_z(jnp.concatenate(slabs, axis=0))
        slabs = rotate(turns.at[1], [lines[i * NG : (i + 1) * NG] for i in range(count)])
        for i, v in enumerate(slabs):
            field[pl.ds(pl.multiple_of(base * PITCH, 8) + i * PITCH, NG), :] = v

    def middle(step, carry):
        group = [step * MROWS + i for i in range(MROWS)]
        slabs = rotate(turns.at[0], [field[pl.ds(at, NG, stride=PITCH), :] for at in group])
        slabs = [v * factor[rows_of(at), :] for at, v in zip(group, slabs)]
        slabs = rotate(turns.at[0], slabs)
        for at, v in zip(group, slabs):
            field[pl.ds(at, NG, stride=PITCH), :] = v
        return carry

    def backward(k, base, count):
        slabs = rotate(turns.at[2], [
            field[pl.ds(pl.multiple_of(base * PITCH, 8) + i * PITCH, NG), :] for i in range(count)
        ])
        lines = along_z(jnp.concatenate(slabs, axis=0))
        for i in range(count):
            rows = rows_of(base + i)
            v = lines[i * NG : (i + 1) * NG] * doubled[rows, :]
            total[rows, :] = jnp.where(k == 0, 0.0, total[rows, :]) - v

    for q in range(CHUNKS):
        swap(q).start()
    target_to(0).start()
    target_to(1).start()

    def keep(i, carry):
        rows = pl.ds(pl.multiple_of(i * PIECE, PIECE), PIECE)
        at = pl.ds(pl.multiple_of(y * half_rows + i * PIECE, PIECE), PIECE)
        held[y, rows, :] = src[at, :]
        return carry

    lax.fori_loop(0, half_rows // PIECE, keep, 0)

    @pl.when(y == 0)
    def _():
        for q in range(CHUNKS):
            inward(0, q).start()

    loads[2].wait()
    off = offsets[grp]

    def flag(value):
        return value.astype(jnp.int32)

    cycle = 2 * planes

    def needs(b, c):
        return flag(lax.rem(b - c - off + 2 * cycle, cycle) < STOPS)

    end = jnp.where(is_end, z, z_out)
    line = []
    for d in range(1, planes):
        p = jnp.where(end == 0, d, planes - 1 - d)
        line += [2 * p, 2 * p + 1]
    skip = jnp.int32(0)
    found = jnp.int32(0)
    for i, c in enumerate(line):
        spare = (1 - found) * (1 - needs(2 * end, c)) * (1 - needs(2 * end + 1, c))
        skip = skip + i * spare
        found = found + spare
    mid_ids = [2 * z, 2 * z + 1, 2 * z_out, 2 * z_in, 2 * z_out + 1, 2 * z_in + 1, 2 * z_far, 2 * z_far + 1]
    end_ids = [2 * z, 2 * z + 1]
    end_ids += [jnp.where(s < skip, line[s], line[s + 1]) for s in range(SLOTS)]

    def places(b):
        rank = jnp.int32(0)
        at = [jnp.int32(0)] * STOPS
        for p, c in enumerate(mid_ids):
            if p < len(end_ids):
                want = needs(b, jnp.where(is_end, end_ids[p], c))
            else:
                want = jnp.where(is_end, 0, needs(b, c))
            for k in range(STOPS):
                at[k] = at[k] + (p - k) * want * flag(rank == k)
            rank = rank + want
        return at

    my_places, buddy_places = places(me), places(buddy)

    def pick(places, k):
        return sum(jnp.where(k == i, places[i], 0) for i in range(STOPS))

    def send_out(s, q):
        first = jnp.where(s < 2, s, jnp.where(s == 2, 3, s + 2))
        second = jnp.where(s + 1 < 2, s + 1, jnp.where(s + 1 == 2, 3, s + 3))
        for i in range(chunk_rows // PIECE):
            rows = pl.ds(pl.multiple_of(q * chunk_rows + i * PIECE, PIECE), PIECE)
            outbox[s, rows, :] = jnp.where(s < skip, held[first, rows, :], held[second, rows, :])
        outward(s, q).start()

    def choose(k, q):
        mine, other = pick(my_places, k), pick(buddy_places, k)
        short = flag(is_end | (k == 0))

        def chosen(which, rows):
            v = held[k, rows, :]
            for j in range(1, STOPS + 1):
                at = k + j - (short if j == STOPS else 0)
                v = jnp.where(which == j, held[at, rows, :], v)
            return v

        for i in range(chunk_rows // PIECE):
            rows = pl.ds(pl.multiple_of(q * chunk_rows + i * PIECE, PIECE), PIECE)
            give[k, rows, :] = chosen(other, rows)
        handing(k, q).start()
        for i in range(chunk_rows // PIECE):
            rows = pl.ds(pl.multiple_of(q * chunk_rows + i * PIECE, PIECE), PIECE)
            at = pl.multiple_of(y * half_rows + q * chunk_rows + i * PIECE, PIECE)
            pool[k, pl.ds(at, PIECE), :] = chosen(mine, rows)

    def open_up(q, carry):
        arrived(1 - y, q)

        @pl.when(y == 1)
        def _():
            inward(0, q).start()

        inward(1, q).start()

        @pl.when(is_mid)
        def _():
            send_out(0, q)

        return carry

    lax.fori_loop(0, CHUNKS, open_up, 0)

    for load in loads[3:]:
        load.wait()
    lax.fori_loop(0, NG // PREP, weigh, 0)

    def target_from(n):
        r = (mate, cross, cross_mate)[n]
        remote(
            tgt, whole.at[quarter(r)], t_send.at[n], t_recv.at[n], to_mate
        ).wait_recv()

    half_planes = NG // 2
    per_chunk = half_planes // CHUNKS

    def forward_own(k):
        def body(i, carry):
            forward(k, y * half_planes + i * FPLANES, FPLANES)
            return carry

        lax.fori_loop(0, half_planes // FPLANES, body, 0)

    def forward_other(k):
        ready = LATE // per_chunk

        def body(i, carry):
            for j in range(ready):
                q = i * ready + j
                remote(
                    give.at[k, part(q)], pool.at[k, part(q, (1 - y) * half_rows)],
                    give_sem.at[k, q], pool_sem.at[k, q], to_buddy,
                ).wait_recv()
            forward(k, (1 - y) * half_planes + i * LATE, LATE)
            return carry

        lax.fori_loop(0, half_planes // LATE, body, 0)

    def near_from(n, i):
        remote(
            over.at[share(0, i)], near.at[n, share(0, i)],
            near_send.at[n, i], near_recv.at[n, i], to_mate,
        ).wait_recv()

    share_planes = NG // 8

    def back(k):
        @pl.when(k < STOPS - 1)
        def _():
            def body(i, carry):
                backward(k, i * BPLANES, BPLANES)
                return carry

            lax.fori_loop(0, NG // BPLANES, body, 0)

        @pl.when(k == STOPS - 1)
        def _():
            def away(i, carry):
                backward(k, (2 * cross_mate + i) * share_planes, share_planes)
                sum_to_mate(0, i).start()
                backward(k, (2 * cross + i) * share_planes, share_planes)
                near_from(0, i)
                across[share(0, i), :] = total[share(cross, i), :] + near[0, share(0, i), :]
                sum_to_cross(i).start()
                return carry

            lax.fori_loop(0, 2, away, 0)

            def home(i, carry):
                r = jnp.where(i == 0, mate, grp)
                backward(k, 2 * r * share_planes, 2 * share_planes)

                @pl.when(i == 0)
                def _():
                    for j in range(2):
                        sum_to_mate(1, j).start()

                return carry

            lax.fori_loop(0, 2, home, 0)

    def step(t, carry):
        def chunk(q, carry):
            @pl.when(is_end & (t < SLOTS))
            def _():
                arrived(2 + t, q)

            @pl.when(is_mid & (t < SLOTS - 1))
            def _():
                arrived(jnp.where(t == 0, 3, t + 4), q)

                @pl.when(t < 2)
                def _():
                    arrived(2 + 2 * t, q)
                    inward(t + 2, q).start()

                send_out(t + 1, q)

            stop = t - flag(is_end)

            @pl.when((stop >= 0) & (stop < STOPS))
            def _():
                choose(stop, q)

            return carry

        def comm(n):
            lax.fori_loop(n * CHUNKS // 4, (n + 1) * CHUNKS // 4, chunk, 0)

        comm(0)

        @pl.when(t == 0)
        def _():
            target_from(1)
            target_to(2).start()

        @pl.when(t >= 2)
        def _():
            forward_other(t - 2)

        comm(1)

        @pl.when(t >= 2)
        def _():
            lax.fori_loop(0, NG // MROWS, middle, 0)

        comm(2)

        @pl.when(t >= 2)
        def _():
            back(t - 2)

        @pl.when(t == 0)
        def _():
            target_from(0)
            target_from(2)
            lax.fori_loop(0, NG // PREP, prepare, 0)

        comm(3)

        @pl.when((t >= 1) & (t < SLOTS))
        def _():
            forward_own(t - 1)

        return carry

    lax.fori_loop(0, STOPS + 2, step, 0)

    for n in range(3):
        target_to(n).wait_send()

    def drain(q, carry):
        swap(q).wait_send()
        for k in range(STOPS):
            handing(k, q).wait_send()
        for s in range(2):
            inward(s, q).wait_send()

        @pl.when(is_mid)
        def _():
            for s in range(2, 4):
                inward(s, q).wait_send()
            for s in range(SLOTS):
                outward(s, q).wait_send()

        return carry

    lax.fori_loop(0, CHUNKS, drain, 0)

    for i in range(2):
        near_from(1, i)
        remote(
            across.at[share(0, i)], over.at[share(0, i)],
            x_send.at[i], x_recv.at[i], to_cross,
        ).wait_recv()
        for j in range(i * share_planes, (i + 1) * share_planes):
            v = total[rows_of(2 * grp * share_planes + j), :] + near[1, rows_of(j), :] + over[rows_of(j), :]
            a, b = interleave(v[:HALF], v[HALF:])
            out[pl.ds(j * NG, HALF, stride=2), :] = a
            out[pl.ds(j * NG + 1, HALF, stride=2), :] = b

    for i in range(2):
        sum_to_cross(i).wait_send()
        for n in range(2):
            sum_to_mate(n, i).wait_send()


def packed_tables():
    along_x, along_y, back_y, z_high, z_low, plane, wave = tables()
    z_high, z_low = z_high[:LANES, :LANES], z_low[:LANES, :LANES]
    z_table = np.block([[z_high, z_low], [z_high, np.zeros_like(z_low)]])
    waves = np.concatenate([plane, np.tile(wave[:, None], (1, LANES))], axis=0)
    return [jnp.asarray(v) for v in (np.stack([along_x, along_y, back_y]), z_table, waves)]


def plane_exchange(offsets, occupation, source, quarter):
    tables = packed_tables()
    rows = source.shape[0]
    half = rows // 2
    part = quarter.shape[0]
    vmem = pl.BlockSpec(memory_space=pltpu.VMEM)
    dma = pltpu.SemaphoreType.DMA
    box = functools.partial(pltpu.VMEM, dtype=jnp.float32)
    return pl.pallas_call(
        exchange_kernel,
        out_shape=jax.ShapeDtypeStruct(quarter.shape, jnp.float32),
        in_specs=[pl.BlockSpec(memory_space=pl.ANY)] * (4 + len(tables)),
        out_specs=vmem,
        scratch_shapes=[
            pltpu.SMEM(offsets.shape, jnp.int32),
            pltpu.SMEM(occupation.shape, jnp.int32),
            *[pltpu.VMEM(v.shape, v.dtype) for v in tables],
            box((rows, LANES)),
            box((8, half, LANES)),
            box((SLOTS, half, LANES)),
            box((STOPS, half, LANES)),
            box((STOPS, rows, LANES)),
            box((NG * NG, LANES)),
            box((NG * NG, LANES)),
            box((NG * NG, LANES)),
            box((NG * NG, LANES)),
            box((NG * NG, LANES)),
            box((NG * PITCH, LANES)),
            box((2, part, LANES)),
            box((part, LANES)),
            box((part, LANES)),
            dma((8, CHUNKS)),
            dma((CHUNKS,)),
            dma((4, CHUNKS)),
            dma((SLOTS, CHUNKS)),
            dma((STOPS, CHUNKS)),
            dma((STOPS, CHUNKS)),
            dma((7,)),
            dma((3,)),
            dma((3,)),
            dma((2, 2)),
            dma((2, 2)),
            dma((2,)),
            dma((2,)),
        ],
        compiler_params=pltpu.CompilerParams(
            vmem_limit_bytes=56 * 1024 * 1024, collective_id=0, has_side_effects=True
        ),
        cost_estimate=pl.CostEstimate(
            flops=40_000_000_000, bytes_accessed=8_000_000, transcendentals=0
        ),
    )(offsets, occupation, source, quarter, *tables)


def ring_order(count):
    return list(range(0, count, 2)) + list(range(1, count, 2))[::-1]


def arrival(count):
    order = ring_order(count)
    place = [order.index(i) for i in range(count)]
    worst = [0] * STOPS
    for b in range(count):
        for off in range(count):
            steps = []
            for k in range(STOPS):
                d = (place[b] - place[(b - off - k) % count]) % count
                steps.append(min(d, count - d))
            worst = [max(w, s) for w, s in zip(worst, sorted(steps))]
    return worst


def partner(value, axis, bit):
    return lax.ppermute(value, axis, [(i, i ^ bit) for i in range(lax.axis_size(axis))])


def gather_rows(quarter, axis):
    me = lax.axis_index(axis)
    count = lax.axis_size(axis)
    parts = {0: quarter}
    bit = count // 2
    while bit:
        for key, value in list(parts.items()):
            parts[key ^ bit] = partner(value, axis, bit)
        bit //= 2
    ordered = []
    keys = sorted(parts)
    level = [parts[k] for k in keys]
    bit = 1
    while bit < count:
        swap = (me // bit) % 2 == 1
        merged = []
        for i in range(0, len(level), 2):
            a, b = level[i], level[i + 1]
            merged.append(
                jnp.concatenate([jnp.where(swap, b, a), jnp.where(swap, a, b)], axis=1)
            )
        level = merged
        bit *= 2
    return level[0]


def scatter_rows(total, axis):
    me = lax.axis_index(axis)
    count = lax.axis_size(axis)
    targets, rows, lanes = total.shape
    value = total.reshape((targets, count, rows // count, lanes))
    bit = 1
    while bit < count:
        mine = (me // bit) % 2 == 1
        pairs = value.reshape((targets, value.shape[1] // 2, 2) + value.shape[2:])
        low, high = pairs[:, :, 0], pairs[:, :, 1]
        value = jnp.where(mine, high, low) + partner(jnp.where(mine, low, high), axis, bit)
        bit *= 2
    return value[:, 0]


def local(targets, sources, occupation, offsets):
    count = lax.axis_size("blk")
    target_count, cells = targets.shape[0], sources.shape[1]
    quarter = targets.reshape(target_count, targets.shape[1] // LANES, LANES)
    if count == 2 * STOPS and lax.axis_size("grp") == 4:
        mixed = quarter.transpose(1, 0, 2).reshape(-1, LANES)
        result = plane_exchange(offsets, occupation, sources.reshape(-1, LANES), mixed)
        return result.reshape(-1, target_count, LANES).transpose(1, 0, 2).reshape(targets.shape)
    consts = [jnp.asarray(v) for v in tables()]
    scale = jnp.sqrt(occupation.astype(jnp.float32) * 0.5)
    scaled = (sources * scale[:, None]).reshape(cells // LANES, LANES)
    whole = gather_rows(quarter, "grp")

    order = ring_order(count)
    up = [(order[i], order[(i + 1) % count]) for i in range(count)]
    down = [(b, a) for a, b in up]
    worst = arrival(count)
    pool = [scaled]
    ahead = behind = scaled
    for step in range(1, count // 2 + 1):
        if step < count // 2:
            ahead = lax.ppermute(ahead, "blk", up)
            behind = lax.ppermute(behind, "blk", down)
            pool += [ahead, behind]
        else:
            half = scaled.shape[0] // 2
            upper = lax.ppermute(ahead[:half], "blk", up)
            lower = lax.ppermute(behind[half:], "blk", down)
            pool += [jnp.concatenate([upper, lower], axis=0)]

    place = np.zeros(count, np.int32)
    place[order] = np.arange(count)
    place = jnp.asarray(place)
    me = lax.axis_index("blk")
    offset = lax.dynamic_index_in_dim(offsets, lax.axis_index("grp"), 0, keepdims=False)
    block = (me - offset - jnp.arange(STOPS, dtype=jnp.int32)) % count
    back = (place[me] - place[block]) % count
    slot = jnp.where(
        back == 0, 0, jnp.where(back <= count // 2, 2 * back - 1, 2 * (count - back))
    ).astype(jnp.int32)
    rank = jnp.sum((slot[None, :] < slot[:, None]).astype(jnp.int32), axis=1)
    ranked = jnp.sum(
        jnp.where(rank[None, :] == jnp.arange(STOPS)[:, None], slot[None, :], 0), axis=1
    ).astype(jnp.int32)

    total = None
    for first, end in CALLS:
        there = pool[: 2 * worst[end - 1] + 1]
        total = exchange_terms(ranked[first:end], there, whole, total, consts)
    return scatter_rows(total, "grp").reshape(targets.shape)


def solution(mesh):
    in_specs = (P("blk", "grp"), P(("grp", "blk"), None), P(("grp", "blk")), P())
    out_specs = P("blk", "grp")
    return jax.shard_map(local, mesh=mesh, in_specs=in_specs, out_specs=out_specs, check_vma=False)
```

```python
import functools
import math

import jax
import jax.numpy as jnp
import numpy as np
from jax import lax
from jax.experimental import pallas as pl
from jax.experimental.pallas import tpu as pltpu
from jax.sharding import PartitionSpec as P

NG = 64
STOPS = 4
LANES = 128

box_length = 16.0
screen_square = 0.25


def split_np(table):
    high = table.astype(jnp.bfloat16)
    low = (table - high.astype(np.float64)).astype(jnp.bfloat16)
    return high, low


def stacked(table):
    high, low = split_np(table)
    return np.concatenate(
        [np.concatenate([high, high], axis=1), np.concatenate([low, low], axis=1)], axis=0
    )


def tables():
    counter = np.arange(NG)
    angle = 2.0 * np.pi * (counter[:, None] * counter[None, :] % NG) / NG
    cas = (np.cos(angle) + np.sin(angle)) / math.sqrt(NG)
    order = np.concatenate([counter[0::2], counter[1::2]])
    along_x = stacked(cas)
    along_y = stacked(cas[:, order])
    back_y = stacked(cas[order, :])
    z_high, z_low = split_np(np.kron(np.eye(4), cas))
    freq = np.where(counter < NG // 2, counter, counter - NG)
    wave = (2.0 * np.pi * freq / box_length) ** 2
    plane = wave[:, None] + np.tile(wave, 2)[None, :] + screen_square
    return along_x, along_y, back_y, z_high, z_low, plane.astype(np.float32), wave.astype(np.float32)


def split(value):
    high = value.astype(jnp.bfloat16)
    low = (value - high.astype(jnp.float32)).astype(jnp.bfloat16)
    return high, low


def left(table, value):
    high, low = split(value)
    both = jnp.dot(
        table, jnp.concatenate([high, low], axis=0), preferred_element_type=jnp.float32
    )
    return both[:NG] + both[NG:]


def right(z_high, z_low, value):
    high, low = split(value)
    dot = functools.partial(jnp.dot, preferred_element_type=jnp.float32)
    return dot(high, z_high) + (dot(low, z_high) + dot(high, z_low))


HALF = NG // 2
XB = 16
YB = 8
CALLS = ((0, 1), (1, 3), (3, 4))


def pair_kernel(count, has_prior, slots, wave, *refs):
    pool = refs[:count]
    refs = refs[count:]
    targets, along_x, along_y, back_y, z_high, z_low, plane = refs[:7]
    refs = refs[7:]
    if has_prior:
        prior, refs = refs[0], refs[1:]
    out, src, field, sems = refs
    ns = src.shape[0]
    xb, yb = XB * 2 // ns, YB * 2 // ns
    width = ns * LANES

    def wide(parts):
        return jnp.concatenate(parts, axis=1) if ns > 1 else parts[0]

    def load(rows):
        return wide([field[s, rows, :] for s in range(ns)])

    def store(rows, v):
        for s in range(ns):
            field[s, rows, :] = v[:, s * LANES : (s + 1) * LANES]

    for s in range(ns):
        for i in range(count):
            @pl.when(slots[s] == i)
            def _():
                pltpu.make_async_copy(pool[i], src.at[s], sems.at[s]).start()
    for s in range(ns):
        pltpu.make_async_copy(pool[0], src.at[s], sems.at[s]).wait()

    first = lax.broadcasted_iota(jnp.int32, (HALF, LANES), 1) < NG

    def interleave(a, b):
        even = jnp.where(first, a, pltpu.roll(b, NG, 1))
        odd = jnp.where(first, pltpu.roll(a, NG, 1), b)
        return even, odd

    def source_rows(s, x):
        v = src[s, pl.ds(pl.multiple_of(x * HALF, HALF), HALF), :]
        even, odd = interleave(v, v)
        return jnp.concatenate([even, odd], axis=0)

    def source_plane(x):
        return wide([source_rows(s, x) for s in range(ns)])

    def forward(step, carry):
        slabs = []
        for k in range(xb):
            x = step * xb + k
            rows = pl.ds(pl.multiple_of(x * HALF, HALF), HALF)
            even, odd = interleave(targets[0, rows, :], targets[1, rows, :])
            t = jnp.concatenate([even, odd], axis=0)
            slabs.append(wide([t] * ns) * source_plane(x))
        lines = right(z_high[:width, :width], z_low[:width, :width], jnp.concatenate(slabs, axis=0))
        for k in range(xb):
            x = step * xb + k
            rows = pl.ds(pl.multiple_of(x * NG, NG), NG)
            store(rows, left(along_y[...], lines[k * NG : (k + 1) * NG]))
        return carry

    def middle(step, carry):
        group = [step * yb + k for k in range(yb)]
        slabs = []
        for y in group:
            rows = pl.ds(y, NG, stride=PITCH)
            slabs.append(load(rows))
        slabs = [left(along_x[...], v) for v in slabs]
        for k, y in enumerate(group):
            factor = (4.0 * math.pi) / (plane[...] + wave[y])
            slabs[k] = slabs[k] * wide([factor] * ns)
        slabs = [left(along_x[...], v) for v in slabs]
        for y, v in zip(group, slabs):
            rows = pl.ds(y, NG, stride=PITCH)
            store(rows, v)
        return carry

    def backward(step, carry):
        slabs = []
        for k in range(xb):
            x = step * xb + k
            rows = pl.ds(pl.multiple_of(x * NG, NG), NG)
            slabs.append(left(back_y[...], load(rows)))
        lines = right(z_high[:width, :width], z_low[:width, :width], jnp.concatenate(slabs, axis=0))
        for k in range(xb):
            x = step * xb + k
            v = lines[k * NG : (k + 1) * NG] * source_plane(x)
            v = sum(v[:, s * LANES : (s + 1) * LANES] for s in range(ns))
            a, b = interleave(v[:HALF], v[HALF:])
            rows = pl.ds(pl.multiple_of(x * HALF, HALF), HALF)
            if has_prior:
                out[0, rows, :] = prior[0, rows, :] - a
                out[1, rows, :] = prior[1, rows, :] - b
            else:
                out[0, rows, :] = -a
                out[1, rows, :] = -b
        return carry

    lax.fori_loop(0, NG // xb, forward, 0)
    lax.fori_loop(0, NG // yb, middle, 0)
    lax.fori_loop(0, NG // xb, backward, 0)


def exchange_terms(slots, pool, targets, prior, consts):
    *mats, wave = consts
    rows = targets.shape[1]
    ns = slots.shape[0]
    smem = pl.BlockSpec(memory_space=pltpu.SMEM)
    vmem = pl.BlockSpec(memory_space=pltpu.VMEM)
    anywhere = pl.BlockSpec(memory_space=pl.ANY)
    extra = [] if prior is None else [prior]
    return pl.pallas_call(
        functools.partial(pair_kernel, len(pool), prior is not None),
        out_shape=jax.ShapeDtypeStruct(targets.shape, jnp.float32),
        in_specs=[smem, smem] + [anywhere] * len(pool) + [vmem] * (1 + len(mats) + len(extra)),
        out_specs=vmem,
        scratch_shapes=[
            pltpu.VMEM((ns, rows, LANES), jnp.float32),
            pltpu.VMEM((ns, NG * NG, LANES), jnp.float32),
            pltpu.SemaphoreType.DMA((ns,)),
        ],
        compiler_params=pltpu.CompilerParams(vmem_limit_bytes=40 * 1024 * 1024),
        cost_estimate=pl.CostEstimate(
            flops=10_000_000_000 * ns, bytes_accessed=8_000_000, transcendentals=0
        ),
    )(slots, wave, *pool, targets, *mats, *extra)


CHUNKS = 8
SLOTS = 5
PIECE = 64
FPLANES = 32
LATE = 16
BPLANES = 32
MROWS = 32
PITCH = 72
PREP = 4
ROOM = 1 << 20


def exchange_kernel(
    offsets_in, electrons_in, raw, tgt, turns_in, z_table_in, waves_in, out,
    offsets, electrons, turns, z_table, waves,
    src, held, outbox, give, pool, whole, paired, factor, doubled, total, field, near, over, across,
    held_sem, a_sem, inner_sem, outer_sem, give_sem, pool_sem,
    local_sem, t_send, t_recv, near_send, near_recv, x_send, x_recv,
):
    planes = lax.axis_size("blk") // 2
    half_rows = src.shape[0] // 2
    chunk_rows = half_rows // CHUNKS
    quarter_rows = tgt.shape[0]
    me, grp = lax.axis_index("blk"), lax.axis_index("grp")
    z, y = me // 2, me % 2
    buddy = 2 * z + 1 - y
    x, core = grp // 2, grp % 2
    mate = 2 * x + 1 - core
    cross = 2 * (1 - x) + core
    cross_mate = 2 * (1 - x) + 1 - core
    is_end = (z == 0) | (z == planes - 1)
    is_mid = jnp.logical_not(is_end)
    z_in = 1 + z % 2
    z_out = (planes - 1) * jnp.maximum(z - 1, 0)
    z_far = planes - 1 - z_out
    to_buddy, to_in = {"blk": buddy}, {"blk": 2 * z_in + y}
    to_out = {"blk": 2 * z_out + y}
    to_mate, to_cross = {"grp": mate}, {"grp": cross}

    def remote(a, b, send, recv, device):
        return pltpu.make_async_remote_copy(
            src_ref=a, dst_ref=b, send_sem=send, recv_sem=recv,
            device_id=device, device_id_type=pl.DeviceIdType.MESH,
        )

    loads = [
        pltpu.make_async_copy(a, b, local_sem.at[i])
        for i, (a, b) in enumerate(
            (
                (raw, src),
                (electrons_in, electrons),
                (offsets_in, offsets),
                (waves_in.at[pl.ds(0, waves.shape[0])], waves),
                (z_table_in.at[pl.ds(0, z_table.shape[0])], z_table),
                (turns_in.at[pl.ds(0, turns.shape[0])], turns),
                (tgt, whole.at[pl.ds(pl.multiple_of(grp * tgt.shape[0], tgt.shape[0]), tgt.shape[0])]),
            )
        )
    ]
    for load in loads:
        load.start()

    barrier = pltpu.get_barrier_semaphore()
    for device in (to_buddy, to_in, to_mate, to_cross):
        pl.semaphore_signal(barrier, inc=1, device_id=device, device_id_type=pl.DeviceIdType.MESH)

    loads[0].wait()
    loads[1].wait()
    scale = jnp.sqrt(jnp.full((PIECE, LANES), electrons[0].astype(jnp.float32) * 0.5))

    def rescale(i, carry):
        rows = pl.ds(pl.multiple_of(i * PIECE, PIECE), PIECE)
        src[rows, :] = src[rows, :] * scale
        return carry

    lax.fori_loop(0, src.shape[0] // PIECE, rescale, 0)

    @pl.when(is_mid)
    def _():
        pl.semaphore_signal(barrier, inc=1, device_id=to_out, device_id_type=pl.DeviceIdType.MESH)
        pl.semaphore_wait(barrier, 5)

    @pl.when(is_end)
    def _():
        pl.semaphore_wait(barrier, 4)

    def part(q, base=0):
        return pl.ds(pl.multiple_of(base + q * chunk_rows, chunk_rows), chunk_rows)

    def swap(q):
        return remote(
            src.at[part(q, (1 - y) * half_rows)], held.at[y, part(q)],
            a_sem.at[q], held_sem.at[y, q], to_buddy,
        )

    def inward(s, q):
        at = jnp.where(s < 2, s, 2 * (s - 1))
        to = jnp.where(is_end, 2 + 2 * s, jnp.where(s == 0, 3, s + 4))
        return remote(
            held.at[at, part(q)], held.at[to, part(q)],
            inner_sem.at[s, q], held_sem.at[to, q], to_in,
        )

    def outward(s, q):
        return remote(
            outbox.at[s, part(q)], held.at[2 + s, part(q)],
            outer_sem.at[s, q], held_sem.at[2 + s, q], to_out,
        )

    def handing(k, q):
        return remote(
            give.at[k, part(q)], pool.at[k, part(q, y * half_rows)],
            give_sem.at[k, q], pool_sem.at[k, q], to_buddy,
        )

    def arrived(p, q):
        remote(
            held.at[p, part(q)], held.at[p, part(q)],
            a_sem.at[q], held_sem.at[p, q], to_buddy,
        ).wait_recv()

    def quarter(r):
        return pl.ds(pl.multiple_of(r * quarter_rows, quarter_rows), quarter_rows)

    def share(r, i):
        n = quarter_rows // 2
        return pl.ds(pl.multiple_of((2 * r + i) * n, n), n)

    def target_to(n):
        if n == 0:
            a, r, device = tgt, grp, to_mate
        elif n == 1:
            a, r, device = tgt, grp, to_cross
        else:
            a, r, device = whole.at[quarter(cross)], cross, to_mate
        return remote(a, whole.at[quarter(r)], t_send.at[n], t_recv.at[n], device)

    def sum_to_mate(n, i):
        r = jnp.where(n == 0, cross_mate, mate)
        return remote(
            total.at[share(r, i)], near.at[n, share(0, i)],
            near_send.at[n, i], near_recv.at[n, i], to_mate,
        )

    def sum_to_cross(i):
        return remote(
            across.at[share(0, i)], over.at[share(0, i)],
            x_send.at[i], x_recv.at[i], to_cross,
        )

    first = lax.broadcasted_iota(jnp.int32, (HALF, LANES), 1) < NG

    def interleave(a, b):
        even = jnp.where(first, a, pltpu.roll(b, NG, 1))
        odd = jnp.where(first, pltpu.roll(a, NG, 1), b)
        return even, odd

    def rows_of(at, n=1):
        return pl.ds(pl.multiple_of(at * NG, NG), n * NG)

    def lines_of(at):
        return pl.ds(pl.multiple_of(at * HALF, HALF), HALF)

    def along_z(value):
        high, low = split(value)
        both = jnp.dot(
            jnp.concatenate([high, low], axis=1), z_table[...], preferred_element_type=jnp.float32
        )
        return both[:, :LANES] + both[:, LANES:]

    def rotate(table, values):
        out = []
        for i in range(0, len(values), 2):
            both = left(table[...], jnp.concatenate(values[i : i + 2], axis=1))
            out += [both[:, :LANES], both[:, LANES:]]
        return out

    def prepare(step, carry):
        for i in range(PREP):
            at = step * PREP + i
            even, odd = interleave(
                whole[pl.ds(at * NG, HALF, stride=2), :], whole[pl.ds(at * NG + 1, HALF, stride=2), :]
            )
            paired[rows_of(at), :] = jnp.concatenate([even, odd], axis=0)
        return carry

    def weigh(step, carry):
        for i in range(PREP):
            at = step * PREP + i
            factor[rows_of(at), :] = (4.0 * math.pi) / (waves[:NG, :] + waves[pl.ds(NG + at, 1), :])
        return carry

    def forward(k, base, count):
        slabs = []
        for i in range(count):
            at = base + i
            v = pool[k, lines_of(at), :]
            even, odd = interleave(v, v)
            v = jnp.concatenate([even, odd], axis=0)
            doubled[rows_of(at), :] = v
            slabs.append(paired[rows_of(at), :] * v)
        lines = along_z(jnp.concatenate(slabs, axis=0))
        slabs = rotate(turns.at[1], [lines[i * NG : (i + 1) * NG] for i in range(count)])
        for i, v in enumerate(slabs):
            field[pl.ds(pl.multiple_of(base * PITCH, 8) + i * PITCH, NG), :] = v

    def middle(step, carry):
        group = [step * MROWS + i for i in range(MROWS)]
        slabs = rotate(turns.at[0], [field[pl.ds(at, NG, stride=PITCH), :] for at in group])
        slabs = [v * factor[rows_of(at), :] for at, v in zip(group, slabs)]
        slabs = rotate(turns.at[0], slabs)
        for at, v in zip(group, slabs):
            field[pl.ds(at, NG, stride=PITCH), :] = v
        return carry

    def backward(k, base, count):
        slabs = rotate(turns.at[2], [
            field[pl.ds(pl.multiple_of(base * PITCH, 8) + i * PITCH, NG), :] for i in range(count)
        ])
        lines = along_z(jnp.concatenate(slabs, axis=0))
        for i in range(count):
            rows = rows_of(base + i)
            v = lines[i * NG : (i + 1) * NG] * doubled[rows, :]
            total[rows, :] = jnp.where(k == 0, 0.0, total[rows, :]) - v

    for q in range(CHUNKS):
        swap(q).start()
    target_to(0).start()
    target_to(1).start()

    def keep(i, carry):
        rows = pl.ds(pl.multiple_of(i * PIECE, PIECE), PIECE)
        at = pl.ds(pl.multiple_of(y * half_rows + i * PIECE, PIECE), PIECE)
        held[y, rows, :] = src[at, :]
        return carry

    lax.fori_loop(0, half_rows // PIECE, keep, 0)

    @pl.when(y == 0)
    def _():
        for q in range(CHUNKS):
            inward(0, q).start()

    loads[2].wait()
    off = offsets[grp]

    def flag(value):
        return value.astype(jnp.int32)

    cycle = 2 * planes

    def needs(b, c):
        return flag(lax.rem(b - c - off + 2 * cycle, cycle) < STOPS)

    end = jnp.where(is_end, z, z_out)
    line = []
    for d in range(1, planes):
        p = jnp.where(end == 0, d, planes - 1 - d)
        line += [2 * p, 2 * p + 1]
    skip = jnp.int32(0)
    found = jnp.int32(0)
    for i, c in enumerate(line):
        spare = (1 - found) * (1 - needs(2 * end, c)) * (1 - needs(2 * end + 1, c))
        skip = skip + i * spare
        found = found + spare
    mid_ids = [2 * z, 2 * z + 1, 2 * z_out, 2 * z_in, 2 * z_out + 1, 2 * z_in + 1, 2 * z_far, 2 * z_far + 1]
    end_ids = [2 * z, 2 * z + 1]
    end_ids += [jnp.where(s < skip, line[s], line[s + 1]) for s in range(SLOTS)]

    def places(b):
        rank = jnp.int32(0)
        at = [jnp.int32(0)] * STOPS
        for p, c in enumerate(mid_ids):
            if p < len(end_ids):
                want = needs(b, jnp.where(is_end, end_ids[p], c))
            else:
                want = jnp.where(is_end, 0, needs(b, c))
            for k in range(STOPS):
                at[k] = at[k] + (p - k) * want * flag(rank == k)
            rank = rank + want
        return at

    my_places, buddy_places = places(me), places(buddy)

    def pick(places, k):
        return sum(jnp.where(k == i, places[i], 0) for i in range(STOPS))

    def send_out(s, q):
        first = jnp.where(s < 2, s, jnp.where(s == 2, 3, s + 2))
        second = jnp.where(s + 1 < 2, s + 1, jnp.where(s + 1 == 2, 3, s + 3))
        for i in range(chunk_rows // PIECE):
            rows = pl.ds(pl.multiple_of(q * chunk_rows + i * PIECE, PIECE), PIECE)
            outbox[s, rows, :] = jnp.where(s < skip, held[first, rows, :], held[second, rows, :])
        outward(s, q).start()

    def choose(k, q):
        mine, other = pick(my_places, k), pick(buddy_places, k)
        short = flag(is_end | (k == 0))

        def chosen(which, rows):
            v = held[k, rows, :]
            for j in range(1, STOPS + 1):
                at = k + j - (short if j == STOPS else 0)
                v = jnp.where(which == j, held[at, rows, :], v)
            return v

        for i in range(chunk_rows // PIECE):
            rows = pl.ds(pl.multiple_of(q * chunk_rows + i * PIECE, PIECE), PIECE)
            give[k, rows, :] = chosen(other, rows)
        handing(k, q).start()
        for i in range(chunk_rows // PIECE):
            rows = pl.ds(pl.multiple_of(q * chunk_rows + i * PIECE, PIECE), PIECE)
            at = pl.multiple_of(y * half_rows + q * chunk_rows + i * PIECE, PIECE)
            pool[k, pl.ds(at, PIECE), :] = chosen(mine, rows)

    def open_up(q, carry):
        arrived(1 - y, q)

        @pl.when(y == 1)
        def _():
            inward(0, q).start()

        inward(1, q).start()

        @pl.when(is_mid)
        def _():
            send_out(0, q)

        return carry

    lax.fori_loop(0, CHUNKS, open_up, 0)

    for load in loads[3:]:
        load.wait()
    lax.fori_loop(0, NG // PREP, weigh, 0)

    def target_from(n):
        r = (mate, cross, cross_mate)[n]
        remote(
            tgt, whole.at[quarter(r)], t_send.at[n], t_recv.at[n], to_mate
        ).wait_recv()

    half_planes = NG // 2
    per_chunk = half_planes // CHUNKS

    def forward_own(k):
        def body(i, carry):
            forward(k, y * half_planes + i * FPLANES, FPLANES)
            return carry

        lax.fori_loop(0, half_planes // FPLANES, body, 0)

    def forward_other(k):
        ready = LATE // per_chunk

        def body(i, carry):
            for j in range(ready):
                q = i * ready + j
                remote(
                    give.at[k, part(q)], pool.at[k, part(q, (1 - y) * half_rows)],
                    give_sem.at[k, q], pool_sem.at[k, q], to_buddy,
                ).wait_recv()
            forward(k, (1 - y) * half_planes + i * LATE, LATE)
            return carry

        lax.fori_loop(0, half_planes // LATE, body, 0)

    def near_from(n, i):
        remote(
            over.at[share(0, i)], near.at[n, share(0, i)],
            near_send.at[n, i], near_recv.at[n, i], to_mate,
        ).wait_recv()

    share_planes = NG // 8

    def back(k):
        @pl.when(k < STOPS - 1)
        def _():
            def body(i, carry):
                backward(k, i * BPLANES, BPLANES)
                return carry

            lax.fori_loop(0, NG // BPLANES, body, 0)

        @pl.when(k == STOPS - 1)
        def _():
            def away(i, carry):
                backward(k, (2 * cross_mate + i) * share_planes, share_planes)
                sum_to_mate(0, i).start()
                backward(k, (2 * cross + i) * share_planes, share_planes)
                near_from(0, i)
                across[share(0, i), :] = total[share(cross, i), :] + near[0, share(0, i), :]
                sum_to_cross(i).start()
                return carry

            lax.fori_loop(0, 2, away, 0)

            def home(i, carry):
                r = jnp.where(i == 0, mate, grp)
                backward(k, 2 * r * share_planes, 2 * share_planes)

                @pl.when(i == 0)
                def _():
                    for j in range(2):
                        sum_to_mate(1, j).start()

                return carry

            lax.fori_loop(0, 2, home, 0)

    def step(t, carry):
        def chunk(q, carry):
            @pl.when(is_end & (t < SLOTS))
            def _():
                arrived(2 + t, q)

            @pl.when(is_mid & (t < SLOTS - 1))
            def _():
                arrived(jnp.where(t == 0, 3, t + 4), q)

                @pl.when(t < 2)
                def _():
                    arrived(2 + 2 * t, q)
                    inward(t + 2, q).start()

                send_out(t + 1, q)

            stop = t - flag(is_end)

            @pl.when((stop >= 0) & (stop < STOPS))
            def _():
                choose(stop, q)

            return carry

        def comm(n):
            lax.fori_loop(n * CHUNKS // 4, (n + 1) * CHUNKS // 4, chunk, 0)

        comm(0)

        @pl.when(t == 0)
        def _():
            target_from(1)
            target_to(2).start()

        @pl.when(t >= 2)
        def _():
            forward_other(t - 2)

        comm(1)

        @pl.when(t >= 2)
        def _():
            lax.fori_loop(0, NG // MROWS, middle, 0)

        comm(2)

        @pl.when(t >= 2)
        def _():
            back(t - 2)

        @pl.when(t == 0)
        def _():
            target_from(0)
            target_from(2)
            lax.fori_loop(0, NG // PREP, prepare, 0)

        comm(3)

        @pl.when((t >= 1) & (t < SLOTS))
        def _():
            forward_own(t - 1)

        return carry

    lax.fori_loop(0, STOPS + 2, step, 0)

    for n in range(3):
        target_to(n).wait_send()

    def drain(q, carry):
        swap(q).wait_send()
        for k in range(STOPS):
            handing(k, q).wait_send()
        for s in range(2):
            inward(s, q).wait_send()

        @pl.when(is_mid)
        def _():
            for s in range(2, 4):
                inward(s, q).wait_send()
            for s in range(SLOTS):
                outward(s, q).wait_send()

        return carry

    lax.fori_loop(0, CHUNKS, drain, 0)

    for i in range(2):
        near_from(1, i)
        remote(
            across.at[share(0, i)], over.at[share(0, i)],
            x_send.at[i], x_recv.at[i], to_cross,
        ).wait_recv()
        for j in range(i * share_planes, (i + 1) * share_planes):
            v = total[rows_of(2 * grp * share_planes + j), :] + near[1, rows_of(j), :] + over[rows_of(j), :]
            a, b = interleave(v[:HALF], v[HALF:])
            out[pl.ds(j * NG, HALF, stride=2), :] = a
            out[pl.ds(j * NG + 1, HALF, stride=2), :] = b

    for i in range(2):
        sum_to_cross(i).wait_send()
        for n in range(2):
            sum_to_mate(n, i).wait_send()


def packed_tables():
    along_x, along_y, back_y, z_high, z_low, plane, wave = tables()
    z_high, z_low = z_high[:LANES, :LANES], z_low[:LANES, :LANES]
    z_table = np.block([[z_high, z_low], [z_high, np.zeros_like(z_low)]])
    waves = np.concatenate([plane, np.tile(wave[:, None], (1, LANES))], axis=0)
    return np.stack([along_x, along_y, back_y]), z_table, waves


def roomy(table):
    count = -(-ROOM // (table.nbytes // table.shape[0]))
    tail = np.zeros((count - table.shape[0],) + table.shape[1:], table.dtype)
    return jnp.asarray(np.concatenate([table, tail], axis=0))


def plane_exchange(offsets, occupation, source, quarter):
    tables = packed_tables()
    rows = source.shape[0]
    half = rows // 2
    part = quarter.shape[0]
    vmem = pl.BlockSpec(memory_space=pltpu.VMEM)
    dma = pltpu.SemaphoreType.DMA
    box = functools.partial(pltpu.VMEM, dtype=jnp.float32)
    return pl.pallas_call(
        exchange_kernel,
        out_shape=jax.ShapeDtypeStruct(quarter.shape, jnp.float32),
        in_specs=[pl.BlockSpec(memory_space=pl.ANY)] * (4 + len(tables)),
        out_specs=vmem,
        scratch_shapes=[
            pltpu.SMEM(offsets.shape, jnp.int32),
            pltpu.SMEM(occupation.shape, jnp.int32),
            *[pltpu.VMEM(v.shape, v.dtype) for v in tables],
            box((rows, LANES)),
            box((8, half, LANES)),
            box((SLOTS, half, LANES)),
            box((STOPS, half, LANES)),
            box((STOPS, rows, LANES)),
            box((NG * NG, LANES)),
            box((NG * NG, LANES)),
            box((NG * NG, LANES)),
            box((NG * NG, LANES)),
            box((NG * NG, LANES)),
            box((NG * PITCH, LANES)),
            box((2, part, LANES)),
            box((part, LANES)),
            box((part, LANES)),
            dma((8, CHUNKS)),
            dma((CHUNKS,)),
            dma((4, CHUNKS)),
            dma((SLOTS, CHUNKS)),
            dma((STOPS, CHUNKS)),
            dma((STOPS, CHUNKS)),
            dma((7,)),
            dma((3,)),
            dma((3,)),
            dma((2, 2)),
            dma((2, 2)),
            dma((2,)),
            dma((2,)),
        ],
        compiler_params=pltpu.CompilerParams(
            vmem_limit_bytes=53 * 1024 * 1024, collective_id=0, has_side_effects=True
        ),
        cost_estimate=pl.CostEstimate(
            flops=40_000_000_000, bytes_accessed=8_000_000, transcendentals=0
        ),
    )(offsets, occupation, source, quarter, *[roomy(v) for v in tables])


def ring_order(count):
    return list(range(0, count, 2)) + list(range(1, count, 2))[::-1]


def arrival(count):
    order = ring_order(count)
    place = [order.index(i) for i in range(count)]
    worst = [0] * STOPS
    for b in range(count):
        for off in range(count):
            steps = []
            for k in range(STOPS):
                d = (place[b] - place[(b - off - k) % count]) % count
                steps.append(min(d, count - d))
            worst = [max(w, s) for w, s in zip(worst, sorted(steps))]
    return worst


def partner(value, axis, bit):
    return lax.ppermute(value, axis, [(i, i ^ bit) for i in range(lax.axis_size(axis))])


def gather_rows(quarter, axis):
    me = lax.axis_index(axis)
    count = lax.axis_size(axis)
    parts = {0: quarter}
    bit = count // 2
    while bit:
        for key, value in list(parts.items()):
            parts[key ^ bit] = partner(value, axis, bit)
        bit //= 2
    ordered = []
    keys = sorted(parts)
    level = [parts[k] for k in keys]
    bit = 1
    while bit < count:
        swap = (me // bit) % 2 == 1
        merged = []
        for i in range(0, len(level), 2):
            a, b = level[i], level[i + 1]
            merged.append(
                jnp.concatenate([jnp.where(swap, b, a), jnp.where(swap, a, b)], axis=1)
            )
        level = merged
        bit *= 2
    return level[0]


def scatter_rows(total, axis):
    me = lax.axis_index(axis)
    count = lax.axis_size(axis)
    targets, rows, lanes = total.shape
    value = total.reshape((targets, count, rows // count, lanes))
    bit = 1
    while bit < count:
        mine = (me // bit) % 2 == 1
        pairs = value.reshape((targets, value.shape[1] // 2, 2) + value.shape[2:])
        low, high = pairs[:, :, 0], pairs[:, :, 1]
        value = jnp.where(mine, high, low) + partner(jnp.where(mine, low, high), axis, bit)
        bit *= 2
    return value[:, 0]


def local(targets, sources, occupation, offsets):
    count = lax.axis_size("blk")
    target_count, cells = targets.shape[0], sources.shape[1]
    quarter = targets.reshape(target_count, targets.shape[1] // LANES, LANES)
    if count == 2 * STOPS and lax.axis_size("grp") == 4:
        mixed = quarter.transpose(1, 0, 2).reshape(-1, LANES)
        result = plane_exchange(offsets, occupation, sources.reshape(-1, LANES), mixed)
        return result.reshape(-1, target_count, LANES).transpose(1, 0, 2).reshape(targets.shape)
    consts = [jnp.asarray(v) for v in tables()]
    scale = jnp.sqrt(occupation.astype(jnp.float32) * 0.5)
    scaled = (sources * scale[:, None]).reshape(cells // LANES, LANES)
    whole = gather_rows(quarter, "grp")

    order = ring_order(count)
    up = [(order[i], order[(i + 1) % count]) for i in range(count)]
    down = [(b, a) for a, b in up]
    worst = arrival(count)
    pool = [scaled]
    ahead = behind = scaled
    for step in range(1, count // 2 + 1):
        if step < count // 2:
            ahead = lax.ppermute(ahead, "blk", up)
            behind = lax.ppermute(behind, "blk", down)
            pool += [ahead, behind]
        else:
            half = scaled.shape[0] // 2
            upper = lax.ppermute(ahead[:half], "blk", up)
            lower = lax.ppermute(behind[half:], "blk", down)
            pool += [jnp.concatenate([upper, lower], axis=0)]

    place = np.zeros(count, np.int32)
    place[order] = np.arange(count)
    place = jnp.asarray(place)
    me = lax.axis_index("blk")
    offset = lax.dynamic_index_in_dim(offsets, lax.axis_index("grp"), 0, keepdims=False)
    block = (me - offset - jnp.arange(STOPS, dtype=jnp.int32)) % count
    back = (place[me] - place[block]) % count
    slot = jnp.where(
        back == 0, 0, jnp.where(back <= count // 2, 2 * back - 1, 2 * (count - back))
    ).astype(jnp.int32)
    rank = jnp.sum((slot[None, :] < slot[:, None]).astype(jnp.int32), axis=1)
    ranked = jnp.sum(
        jnp.where(rank[None, :] == jnp.arange(STOPS)[:, None], slot[None, :], 0), axis=1
    ).astype(jnp.int32)

    total = None
    for first, end in CALLS:
        there = pool[: 2 * worst[end - 1] + 1]
        total = exchange_terms(ranked[first:end], there, whole, total, consts)
    return scatter_rows(total, "grp").reshape(targets.shape)


def solution(mesh):
    in_specs = (P("blk", "grp"), P(("grp", "blk"), None), P(("grp", "blk")), P())
    out_specs = P("blk", "grp")
    return jax.shard_map(local, mesh=mesh, in_specs=in_specs, out_specs=out_specs, check_vma=False)
```

```python
import functools
import math

import jax
import jax.numpy as jnp
import numpy as np
from jax import lax
from jax.experimental import pallas as pl
from jax.experimental.pallas import tpu as pltpu
from jax.sharding import PartitionSpec as P

NG = 64
STOPS = 4
LANES = 128

box_length = 16.0
screen_square = 0.25


def split_np(table):
    high = table.astype(jnp.bfloat16)
    low = (table - high.astype(np.float64)).astype(jnp.bfloat16)
    return high, low


def stacked(table):
    high, low = split_np(table)
    return np.concatenate(
        [np.concatenate([high, high], axis=1), np.concatenate([low, low], axis=1)], axis=0
    )


def tables():
    counter = np.arange(NG)
    angle = 2.0 * np.pi * (counter[:, None] * counter[None, :] % NG) / NG
    cas = (np.cos(angle) + np.sin(angle)) / math.sqrt(NG)
    order = np.concatenate([counter[0::2], counter[1::2]])
    along_x = stacked(cas)
    along_y = stacked(cas[:, order])
    back_y = stacked(cas[order, :])
    z_high, z_low = split_np(np.kron(np.eye(4), cas))
    freq = np.where(counter < NG // 2, counter, counter - NG)
    wave = (2.0 * np.pi * freq / box_length) ** 2
    plane = wave[:, None] + np.tile(wave, 2)[None, :] + screen_square
    return along_x, along_y, back_y, z_high, z_low, plane.astype(np.float32), wave.astype(np.float32)


def split(value):
    high = value.astype(jnp.bfloat16)
    low = (value - high.astype(jnp.float32)).astype(jnp.bfloat16)
    return high, low


def left(table, value):
    high, low = split(value)
    both = jnp.dot(
        table, jnp.concatenate([high, low], axis=0), preferred_element_type=jnp.float32
    )
    return both[:NG] + both[NG:]


def right(z_high, z_low, value):
    high, low = split(value)
    dot = functools.partial(jnp.dot, preferred_element_type=jnp.float32)
    return dot(high, z_high) + (dot(low, z_high) + dot(high, z_low))


HALF = NG // 2
XB = 16
YB = 8
CALLS = ((0, 1), (1, 3), (3, 4))


def pair_kernel(count, has_prior, slots, wave, *refs):
    pool = refs[:count]
    refs = refs[count:]
    targets, along_x, along_y, back_y, z_high, z_low, plane = refs[:7]
    refs = refs[7:]
    if has_prior:
        prior, refs = refs[0], refs[1:]
    out, src, field, sems = refs
    ns = src.shape[0]
    xb, yb = XB * 2 // ns, YB * 2 // ns
    width = ns * LANES

    def wide(parts):
        return jnp.concatenate(parts, axis=1) if ns > 1 else parts[0]

    def load(rows):
        return wide([field[s, rows, :] for s in range(ns)])

    def store(rows, v):
        for s in range(ns):
            field[s, rows, :] = v[:, s * LANES : (s + 1) * LANES]

    for s in range(ns):
        for i in range(count):
            @pl.when(slots[s] == i)
            def _():
                pltpu.make_async_copy(pool[i], src.at[s], sems.at[s]).start()
    for s in range(ns):
        pltpu.make_async_copy(pool[0], src.at[s], sems.at[s]).wait()

    first = lax.broadcasted_iota(jnp.int32, (HALF, LANES), 1) < NG

    def interleave(a, b):
        even = jnp.where(first, a, pltpu.roll(b, NG, 1))
        odd = jnp.where(first, pltpu.roll(a, NG, 1), b)
        return even, odd

    def source_rows(s, x):
        v = src[s, pl.ds(pl.multiple_of(x * HALF, HALF), HALF), :]
        even, odd = interleave(v, v)
        return jnp.concatenate([even, odd], axis=0)

    def source_plane(x):
        return wide([source_rows(s, x) for s in range(ns)])

    def forward(step, carry):
        slabs = []
        for k in range(xb):
            x = step * xb + k
            rows = pl.ds(pl.multiple_of(x * HALF, HALF), HALF)
            even, odd = interleave(targets[0, rows, :], targets[1, rows, :])
            t = jnp.concatenate([even, odd], axis=0)
            slabs.append(wide([t] * ns) * source_plane(x))
        lines = right(z_high[:width, :width], z_low[:width, :width], jnp.concatenate(slabs, axis=0))
        for k in range(xb):
            x = step * xb + k
            rows = pl.ds(pl.multiple_of(x * NG, NG), NG)
            store(rows, left(along_y[...], lines[k * NG : (k + 1) * NG]))
        return carry

    def middle(step, carry):
        group = [step * yb + k for k in range(yb)]
        slabs = []
        for y in group:
            rows = pl.ds(y, NG, stride=PITCH)
            slabs.append(load(rows))
        slabs = [left(along_x[...], v) for v in slabs]
        for k, y in enumerate(group):
            factor = (4.0 * math.pi) / (plane[...] + wave[y])
            slabs[k] = slabs[k] * wide([factor] * ns)
        slabs = [left(along_x[...], v) for v in slabs]
        for y, v in zip(group, slabs):
            rows = pl.ds(y, NG, stride=PITCH)
            store(rows, v)
        return carry

    def backward(step, carry):
        slabs = []
        for k in range(xb):
            x = step * xb + k
            rows = pl.ds(pl.multiple_of(x * NG, NG), NG)
            slabs.append(left(back_y[...], load(rows)))
        lines = right(z_high[:width, :width], z_low[:width, :width], jnp.concatenate(slabs, axis=0))
        for k in range(xb):
            x = step * xb + k
            v = lines[k * NG : (k + 1) * NG] * source_plane(x)
            v = sum(v[:, s * LANES : (s + 1) * LANES] for s in range(ns))
            a, b = interleave(v[:HALF], v[HALF:])
            rows = pl.ds(pl.multiple_of(x * HALF, HALF), HALF)
            if has_prior:
                out[0, rows, :] = prior[0, rows, :] - a
                out[1, rows, :] = prior[1, rows, :] - b
            else:
                out[0, rows, :] = -a
                out[1, rows, :] = -b
        return carry

    lax.fori_loop(0, NG // xb, forward, 0)
    lax.fori_loop(0, NG // yb, middle, 0)
    lax.fori_loop(0, NG // xb, backward, 0)


def exchange_terms(slots, pool, targets, prior, consts):
    *mats, wave = consts
    rows = targets.shape[1]
    ns = slots.shape[0]
    smem = pl.BlockSpec(memory_space=pltpu.SMEM)
    vmem = pl.BlockSpec(memory_space=pltpu.VMEM)
    anywhere = pl.BlockSpec(memory_space=pl.ANY)
    extra = [] if prior is None else [prior]
    return pl.pallas_call(
        functools.partial(pair_kernel, len(pool), prior is not None),
        out_shape=jax.ShapeDtypeStruct(targets.shape, jnp.float32),
        in_specs=[smem, smem] + [anywhere] * len(pool) + [vmem] * (1 + len(mats) + len(extra)),
        out_specs=vmem,
        scratch_shapes=[
            pltpu.VMEM((ns, rows, LANES), jnp.float32),
            pltpu.VMEM((ns, NG * NG, LANES), jnp.float32),
            pltpu.SemaphoreType.DMA((ns,)),
        ],
        compiler_params=pltpu.CompilerParams(vmem_limit_bytes=40 * 1024 * 1024),
        cost_estimate=pl.CostEstimate(
            flops=10_000_000_000 * ns, bytes_accessed=8_000_000, transcendentals=0
        ),
    )(slots, wave, *pool, targets, *mats, *extra)


CHUNKS = 8
SLOTS = 5
PIECE = 64
FPLANES = 32
LATE = 8
BPLANES = 32
MROWS = 32
PITCH = 72
PREP = 4
SHARES = 4
ROOM = 1 << 20


def exchange_kernel(
    offsets_in, electrons_in, raw, tgt, turns_in, z_table_in, waves_in, out,
    offsets, electrons, turns, z_table, waves,
    src, held, outbox, give, pool, whole, paired, factor, doubled, total, field, near, over, across,
    held_sem, a_sem, inner_sem, outer_sem, give_sem, pool_sem,
    local_sem, t_send, t_recv, near_send, near_recv, x_send, x_recv,
):
    planes = lax.axis_size("blk") // 2
    half_rows = src.shape[0] // 2
    chunk_rows = half_rows // CHUNKS
    quarter_rows = tgt.shape[0]
    me, grp = lax.axis_index("blk"), lax.axis_index("grp")
    z, y = me // 2, me % 2
    buddy = 2 * z + 1 - y
    x, core = grp // 2, grp % 2
    mate = 2 * x + 1 - core
    cross = 2 * (1 - x) + core
    cross_mate = 2 * (1 - x) + 1 - core
    is_end = (z == 0) | (z == planes - 1)
    is_mid = jnp.logical_not(is_end)
    z_in = 1 + z % 2
    z_out = (planes - 1) * jnp.maximum(z - 1, 0)
    z_far = planes - 1 - z_out
    to_buddy, to_in = {"blk": buddy}, {"blk": 2 * z_in + y}
    to_out = {"blk": 2 * z_out + y}
    to_mate, to_cross = {"grp": mate}, {"grp": cross}

    def remote(a, b, send, recv, device):
        return pltpu.make_async_remote_copy(
            src_ref=a, dst_ref=b, send_sem=send, recv_sem=recv,
            device_id=device, device_id_type=pl.DeviceIdType.MESH,
        )

    loads = [
        pltpu.make_async_copy(a, b, local_sem.at[i])
        for i, (a, b) in enumerate(
            (
                (raw, src),
                (electrons_in, electrons),
                (offsets_in, offsets),
                (waves_in.at[pl.ds(0, waves.shape[0])], waves),
                (z_table_in.at[pl.ds(0, z_table.shape[0])], z_table),
                (turns_in.at[pl.ds(0, turns.shape[0])], turns),
                (tgt, whole.at[pl.ds(pl.multiple_of(grp * tgt.shape[0], tgt.shape[0]), tgt.shape[0])]),
            )
        )
    ]
    for load in loads:
        load.start()

    barrier = pltpu.get_barrier_semaphore()
    for device in (to_buddy, to_in, to_mate, to_cross):
        pl.semaphore_signal(barrier, inc=1, device_id=device, device_id_type=pl.DeviceIdType.MESH)

    loads[0].wait()
    loads[1].wait()
    scale = jnp.sqrt(jnp.full((PIECE, LANES), electrons[0].astype(jnp.float32) * 0.5))

    def rescale(i, carry):
        rows = pl.ds(pl.multiple_of(i * PIECE, PIECE), PIECE)
        src[rows, :] = src[rows, :] * scale
        return carry

    lax.fori_loop(0, src.shape[0] // PIECE, rescale, 0)

    @pl.when(is_mid)
    def _():
        pl.semaphore_signal(barrier, inc=1, device_id=to_out, device_id_type=pl.DeviceIdType.MESH)
        pl.semaphore_wait(barrier, 5)

    @pl.when(is_end)
    def _():
        pl.semaphore_wait(barrier, 4)

    def part(q, base=0):
        return pl.ds(pl.multiple_of(base + q * chunk_rows, chunk_rows), chunk_rows)

    def swap(q):
        return remote(
            src.at[part(q, (1 - y) * half_rows)], held.at[y, part(q)],
            a_sem.at[q], held_sem.at[y, q], to_buddy,
        )

    def inward(s, q):
        at = jnp.where(s < 2, s, 2 * (s - 1))
        to = jnp.where(is_end, 2 + 2 * s, jnp.where(s == 0, 3, s + 4))
        return remote(
            held.at[at, part(q)], held.at[to, part(q)],
            inner_sem.at[s, q], held_sem.at[to, q], to_in,
        )

    def outward(s, q):
        return remote(
            outbox.at[s, part(q)], held.at[2 + s, part(q)],
            outer_sem.at[s, q], held_sem.at[2 + s, q], to_out,
        )

    def handing(k, q):
        return remote(
            give.at[k, part(q)], pool.at[k, part(q, y * half_rows)],
            give_sem.at[k, q], pool_sem.at[k, q], to_buddy,
        )

    def arrived(p, q):
        remote(
            held.at[p, part(q)], held.at[p, part(q)],
            a_sem.at[q], held_sem.at[p, q], to_buddy,
        ).wait_recv()

    def quarter(r):
        return pl.ds(pl.multiple_of(r * quarter_rows, quarter_rows), quarter_rows)

    def share(r, i):
        n = quarter_rows // SHARES
        return pl.ds(pl.multiple_of((SHARES * r + i) * n, n), n)

    def target_to(n):
        if n == 0:
            a, r, device = tgt, grp, to_mate
        elif n == 1:
            a, r, device = tgt, grp, to_cross
        else:
            a, r, device = whole.at[quarter(cross)], cross, to_mate
        return remote(a, whole.at[quarter(r)], t_send.at[n], t_recv.at[n], device)

    def sum_to_mate(n, i):
        r = jnp.where(n == 0, cross_mate, mate)
        return remote(
            total.at[share(r, i)], near.at[n, share(0, i)],
            near_send.at[n, i], near_recv.at[n, i], to_mate,
        )

    def sum_to_cross(i):
        return remote(
            across.at[share(0, i)], over.at[share(0, i)],
            x_send.at[i], x_recv.at[i], to_cross,
        )

    first = lax.broadcasted_iota(jnp.int32, (HALF, LANES), 1) < NG

    def interleave(a, b):
        even = jnp.where(first, a, pltpu.roll(b, NG, 1))
        odd = jnp.where(first, pltpu.roll(a, NG, 1), b)
        return even, odd

    def rows_of(at, n=1):
        return pl.ds(pl.multiple_of(at * NG, NG), n * NG)

    def lines_of(at):
        return pl.ds(pl.multiple_of(at * HALF, HALF), HALF)

    def along_z(value):
        high, low = split(value)
        both = jnp.dot(
            jnp.concatenate([high, low], axis=1), z_table[...], preferred_element_type=jnp.float32
        )
        return both[:, :LANES] + both[:, LANES:]

    def rotate(table, values):
        out = []
        for i in range(0, len(values), 2):
            both = left(table[...], jnp.concatenate(values[i : i + 2], axis=1))
            out += [both[:, :LANES], both[:, LANES:]]
        return out

    def prepare(step, carry):
        for i in range(PREP):
            at = step * PREP + i
            even, odd = interleave(
                whole[pl.ds(at * NG, HALF, stride=2), :], whole[pl.ds(at * NG + 1, HALF, stride=2), :]
            )
            paired[rows_of(at), :] = jnp.concatenate([even, odd], axis=0)
        return carry

    def weigh(step, carry):
        for i in range(PREP):
            at = step * PREP + i
            factor[rows_of(at), :] = (4.0 * math.pi) / (waves[:NG, :] + waves[pl.ds(NG + at, 1), :])
        return carry

    def forward(k, base, count):
        slabs = []
        for i in range(count):
            at = base + i
            v = pool[k, lines_of(at), :]
            even, odd = interleave(v, v)
            v = jnp.concatenate([even, odd], axis=0)
            doubled[rows_of(at), :] = v
            slabs.append(paired[rows_of(at), :] * v)
        lines = along_z(jnp.concatenate(slabs, axis=0))
        slabs = rotate(turns.at[1], [lines[i * NG : (i + 1) * NG] for i in range(count)])
        for i, v in enumerate(slabs):
            field[pl.ds(pl.multiple_of(base * PITCH, 8) + i * PITCH, NG), :] = v

    def middle(step, carry):
        group = [step * MROWS + i for i in range(MROWS)]
        slabs = rotate(turns.at[0], [field[pl.ds(at, NG, stride=PITCH), :] for at in group])
        slabs = [v * factor[rows_of(at), :] for at, v in zip(group, slabs)]
        slabs = rotate(turns.at[0], slabs)
        for at, v in zip(group, slabs):
            field[pl.ds(at, NG, stride=PITCH), :] = v
        return carry

    def backward(k, base, count):
        slabs = rotate(turns.at[2], [
            field[pl.ds(pl.multiple_of(base * PITCH, 8) + i * PITCH, NG), :] for i in range(count)
        ])
        lines = along_z(jnp.concatenate(slabs, axis=0))
        for i in range(count):
            rows = rows_of(base + i)
            v = lines[i * NG : (i + 1) * NG] * doubled[rows, :]
            total[rows, :] = jnp.where(k == 0, 0.0, total[rows, :]) - v

    for q in range(CHUNKS):
        swap(q).start()
    target_to(0).start()
    target_to(1).start()

    def keep(i, carry):
        rows = pl.ds(pl.multiple_of(i * PIECE, PIECE), PIECE)
        at = pl.ds(pl.multiple_of(y * half_rows + i * PIECE, PIECE), PIECE)
        held[y, rows, :] = src[at, :]
        return carry

    lax.fori_loop(0, half_rows // PIECE, keep, 0)

    @pl.when(y == 0)
    def _():
        for q in range(CHUNKS):
            inward(0, q).start()

    loads[2].wait()
    off = offsets[grp]

    def flag(value):
        return value.astype(jnp.int32)

    cycle = 2 * planes

    def needs(b, c):
        return flag(lax.rem(b - c - off + 2 * cycle, cycle) < STOPS)

    end = jnp.where(is_end, z, z_out)
    line = []
    for d in range(1, planes):
        p = jnp.where(end == 0, d, planes - 1 - d)
        line += [2 * p, 2 * p + 1]
    skip = jnp.int32(0)
    found = jnp.int32(0)
    for i, c in enumerate(line):
        spare = (1 - found) * (1 - needs(2 * end, c)) * (1 - needs(2 * end + 1, c))
        skip = skip + i * spare
        found = found + spare
    mid_ids = [2 * z, 2 * z + 1, 2 * z_out, 2 * z_in, 2 * z_out + 1, 2 * z_in + 1, 2 * z_far, 2 * z_far + 1]
    end_ids = [2 * z, 2 * z + 1]
    end_ids += [jnp.where(s < skip, line[s], line[s + 1]) for s in range(SLOTS)]

    def places(b):
        rank = jnp.int32(0)
        at = [jnp.int32(0)] * STOPS
        for p, c in enumerate(mid_ids):
            if p < len(end_ids):
                want = needs(b, jnp.where(is_end, end_ids[p], c))
            else:
                want = jnp.where(is_end, 0, needs(b, c))
            for k in range(STOPS):
                at[k] = at[k] + (p - k) * want * flag(rank == k)
            rank = rank + want
        return at

    my_places, buddy_places = places(me), places(buddy)

    def pick(places, k):
        return sum(jnp.where(k == i, places[i], 0) for i in range(STOPS))

    def send_out(s, q):
        first = jnp.where(s < 2, s, jnp.where(s == 2, 3, s + 2))
        second = jnp.where(s + 1 < 2, s + 1, jnp.where(s + 1 == 2, 3, s + 3))
        for i in range(chunk_rows // PIECE):
            rows = pl.ds(pl.multiple_of(q * chunk_rows + i * PIECE, PIECE), PIECE)
            outbox[s, rows, :] = jnp.where(s < skip, held[first, rows, :], held[second, rows, :])
        outward(s, q).start()

    def choose(k, q):
        mine, other = pick(my_places, k), pick(buddy_places, k)
        short = flag(is_end | (k == 0))

        def chosen(which, rows):
            v = held[k, rows, :]
            for j in range(1, STOPS + 1):
                at = k + j - (short if j == STOPS else 0)
                v = jnp.where(which == j, held[at, rows, :], v)
            return v

        for i in range(chunk_rows // PIECE):
            rows = pl.ds(pl.multiple_of(q * chunk_rows + i * PIECE, PIECE), PIECE)
            give[k, rows, :] = chosen(other, rows)
        handing(k, q).start()
        for i in range(chunk_rows // PIECE):
            rows = pl.ds(pl.multiple_of(q * chunk_rows + i * PIECE, PIECE), PIECE)
            at = pl.multiple_of(y * half_rows + q * chunk_rows + i * PIECE, PIECE)
            pool[k, pl.ds(at, PIECE), :] = chosen(mine, rows)

    def open_up(q, carry):
        arrived(1 - y, q)

        @pl.when(y == 1)
        def _():
            inward(0, q).start()

        inward(1, q).start()

        @pl.when(is_mid)
        def _():
            send_out(0, q)

        return carry

    lax.fori_loop(0, CHUNKS, open_up, 0)

    for load in loads[3:]:
        load.wait()
    lax.fori_loop(0, NG // PREP, weigh, 0)

    def target_from(n):
        r = (mate, cross, cross_mate)[n]
        remote(
            tgt, whole.at[quarter(r)], t_send.at[n], t_recv.at[n], to_mate
        ).wait_recv()

    half_planes = NG // 2
    per_chunk = half_planes // CHUNKS

    def forward_own(k):
        def body(i, carry):
            forward(k, y * half_planes + i * FPLANES, FPLANES)
            return carry

        lax.fori_loop(0, half_planes // FPLANES, body, 0)

    def forward_other(k):
        ready = LATE // per_chunk

        def body(i, carry):
            for j in range(ready):
                q = i * ready + j
                remote(
                    give.at[k, part(q)], pool.at[k, part(q, (1 - y) * half_rows)],
                    give_sem.at[k, q], pool_sem.at[k, q], to_buddy,
                ).wait_recv()
            forward(k, (1 - y) * half_planes + i * LATE, LATE)
            return carry

        lax.fori_loop(0, half_planes // LATE, body, 0)

    def near_from(n, i):
        remote(
            over.at[share(0, i)], near.at[n, share(0, i)],
            near_send.at[n, i], near_recv.at[n, i], to_mate,
        ).wait_recv()

    share_planes = NG // 4 // SHARES

    def back(k):
        @pl.when(k < STOPS - 1)
        def _():
            def body(i, carry):
                backward(k, i * BPLANES, BPLANES)
                return carry

            lax.fori_loop(0, NG // BPLANES, body, 0)

        @pl.when(k == STOPS - 1)
        def _():
            def away(i, carry):
                backward(k, (SHARES * cross_mate + i) * share_planes, share_planes)
                sum_to_mate(0, i).start()
                backward(k, (SHARES * cross + i) * share_planes, share_planes)
                near_from(0, i)
                across[share(0, i), :] = total[share(cross, i), :] + near[0, share(0, i), :]
                sum_to_cross(i).start()
                return carry

            lax.fori_loop(0, SHARES, away, 0)

            def home(i, carry):
                r = jnp.where(i == 0, mate, grp)
                backward(k, r * (NG // 4), NG // 4)

                @pl.when(i == 0)
                def _():
                    for j in range(SHARES):
                        sum_to_mate(1, j).start()

                return carry

            lax.fori_loop(0, 2, home, 0)

    def step(t, carry):
        def chunk(q, carry):
            @pl.when(is_end & (t < SLOTS))
            def _():
                arrived(2 + t, q)

            @pl.when(is_mid & (t < SLOTS - 1))
            def _():
                arrived(jnp.where(t == 0, 3, t + 4), q)

                @pl.when(t < 2)
                def _():
                    arrived(2 + 2 * t, q)
                    inward(t + 2, q).start()

                send_out(t + 1, q)

            stop = t - flag(is_end)

            @pl.when((stop >= 0) & (stop < STOPS))
            def _():
                choose(stop, q)

            return carry

        def comm(n):
            lax.fori_loop(n * CHUNKS // 4, (n + 1) * CHUNKS // 4, chunk, 0)

        comm(0)

        @pl.when(t == 0)
        def _():
            target_from(1)
            target_to(2).start()

        @pl.when(t >= 2)
        def _():
            forward_other(t - 2)

        comm(1)

        @pl.when(t >= 2)
        def _():
            lax.fori_loop(0, NG // MROWS, middle, 0)

        comm(2)

        @pl.when(t >= 2)
        def _():
            back(t - 2)

        @pl.when(t == 0)
        def _():
            target_from(0)
            target_from(2)
            lax.fori_loop(0, NG // PREP, prepare, 0)

        comm(3)

        @pl.when((t >= 1) & (t < SLOTS))
        def _():
            forward_own(t - 1)

        return carry

    lax.fori_loop(0, STOPS + 2, step, 0)

    for n in range(3):
        target_to(n).wait_send()

    def drain(q, carry):
        swap(q).wait_send()
        for k in range(STOPS):
            handing(k, q).wait_send()
        for s in range(2):
            inward(s, q).wait_send()

        @pl.when(is_mid)
        def _():
            for s in range(2, 4):
                inward(s, q).wait_send()
            for s in range(SLOTS):
                outward(s, q).wait_send()

        return carry

    lax.fori_loop(0, CHUNKS, drain, 0)

    for i in range(SHARES):
        near_from(1, i)
        remote(
            across.at[share(0, i)], over.at[share(0, i)],
            x_send.at[i], x_recv.at[i], to_cross,
        ).wait_recv()
        for j in range(i * share_planes, (i + 1) * share_planes):
            v = total[rows_of(grp * (NG // 4) + j), :] + near[1, rows_of(j), :] + over[rows_of(j), :]
            a, b = interleave(v[:HALF], v[HALF:])
            out[pl.ds(j * NG, HALF, stride=2), :] = a
            out[pl.ds(j * NG + 1, HALF, stride=2), :] = b

    for i in range(SHARES):
        sum_to_cross(i).wait_send()
        for n in range(2):
            sum_to_mate(n, i).wait_send()


def packed_tables():
    along_x, along_y, back_y, z_high, z_low, plane, wave = tables()
    z_high, z_low = z_high[:LANES, :LANES], z_low[:LANES, :LANES]
    z_table = np.block([[z_high, z_low], [z_high, np.zeros_like(z_low)]])
    waves = np.concatenate([plane, np.tile(wave[:, None], (1, LANES))], axis=0)
    return np.stack([along_x, along_y, back_y]), z_table, waves


def roomy(table):
    count = -(-ROOM // (table.nbytes // table.shape[0]))
    tail = np.zeros((count - table.shape[0],) + table.shape[1:], table.dtype)
    return jnp.asarray(np.concatenate([table, tail], axis=0))


def plane_exchange(offsets, occupation, source, quarter):
    tables = packed_tables()
    rows = source.shape[0]
    half = rows // 2
    part = quarter.shape[0]
    vmem = pl.BlockSpec(memory_space=pltpu.VMEM)
    dma = pltpu.SemaphoreType.DMA
    box = functools.partial(pltpu.VMEM, dtype=jnp.float32)
    return pl.pallas_call(
        exchange_kernel,
        out_shape=jax.ShapeDtypeStruct(quarter.shape, jnp.float32),
        in_specs=[pl.BlockSpec(memory_space=pl.ANY)] * (4 + len(tables)),
        out_specs=vmem,
        scratch_shapes=[
            pltpu.SMEM(offsets.shape, jnp.int32),
            pltpu.SMEM(occupation.shape, jnp.int32),
            *[pltpu.VMEM(v.shape, v.dtype) for v in tables],
            box((rows, LANES)),
            box((8, half, LANES)),
            box((SLOTS, half, LANES)),
            box((STOPS, half, LANES)),
            box((STOPS, rows, LANES)),
            box((NG * NG, LANES)),
            box((NG * NG, LANES)),
            box((NG * NG, LANES)),
            box((NG * NG, LANES)),
            box((NG * NG, LANES)),
            box((NG * PITCH, LANES)),
            box((2, part, LANES)),
            box((part, LANES)),
            box((part, LANES)),
            dma((8, CHUNKS)),
            dma((CHUNKS,)),
            dma((4, CHUNKS)),
            dma((SLOTS, CHUNKS)),
            dma((STOPS, CHUNKS)),
            dma((STOPS, CHUNKS)),
            dma((7,)),
            dma((3,)),
            dma((3,)),
            dma((2, SHARES)),
            dma((2, SHARES)),
            dma((SHARES,)),
            dma((SHARES,)),
        ],
        compiler_params=pltpu.CompilerParams(
            vmem_limit_bytes=53 * 1024 * 1024, collective_id=0, has_side_effects=True
        ),
        cost_estimate=pl.CostEstimate(
            flops=40_000_000_000, bytes_accessed=8_000_000, transcendentals=0
        ),
    )(offsets, occupation, source, quarter, *[roomy(v) for v in tables])


def ring_order(count):
    return list(range(0, count, 2)) + list(range(1, count, 2))[::-1]


def arrival(count):
    order = ring_order(count)
    place = [order.index(i) for i in range(count)]
    worst = [0] * STOPS
    for b in range(count):
        for off in range(count):
            steps = []
            for k in range(STOPS):
                d = (place[b] - place[(b - off - k) % count]) % count
                steps.append(min(d, count - d))
            worst = [max(w, s) for w, s in zip(worst, sorted(steps))]
    return worst


def partner(value, axis, bit):
    return lax.ppermute(value, axis, [(i, i ^ bit) for i in range(lax.axis_size(axis))])


def gather_rows(quarter, axis):
    me = lax.axis_index(axis)
    count = lax.axis_size(axis)
    parts = {0: quarter}
    bit = count // 2
    while bit:
        for key, value in list(parts.items()):
            parts[key ^ bit] = partner(value, axis, bit)
        bit //= 2
    ordered = []
    keys = sorted(parts)
    level = [parts[k] for k in keys]
    bit = 1
    while bit < count:
        swap = (me // bit) % 2 == 1
        merged = []
        for i in range(0, len(level), 2):
            a, b = level[i], level[i + 1]
            merged.append(
                jnp.concatenate([jnp.where(swap, b, a), jnp.where(swap, a, b)], axis=1)
            )
        level = merged
        bit *= 2
    return level[0]


def scatter_rows(total, axis):
    me = lax.axis_index(axis)
    count = lax.axis_size(axis)
    targets, rows, lanes = total.shape
    value = total.reshape((targets, count, rows // count, lanes))
    bit = 1
    while bit < count:
        mine = (me // bit) % 2 == 1
        pairs = value.reshape((targets, value.shape[1] // 2, 2) + value.shape[2:])
        low, high = pairs[:, :, 0], pairs[:, :, 1]
        value = jnp.where(mine, high, low) + partner(jnp.where(mine, low, high), axis, bit)
        bit *= 2
    return value[:, 0]


def local(targets, sources, occupation, offsets):
    count = lax.axis_size("blk")
    target_count, cells = targets.shape[0], sources.shape[1]
    quarter = targets.reshape(target_count, targets.shape[1] // LANES, LANES)
    if count == 2 * STOPS and lax.axis_size("grp") == 4:
        mixed = quarter.transpose(1, 0, 2).reshape(-1, LANES)
        result = plane_exchange(offsets, occupation, sources.reshape(-1, LANES), mixed)
        return result.reshape(-1, target_count, LANES).transpose(1, 0, 2).reshape(targets.shape)
    consts = [jnp.asarray(v) for v in tables()]
    scale = jnp.sqrt(occupation.astype(jnp.float32) * 0.5)
    scaled = (sources * scale[:, None]).reshape(cells // LANES, LANES)
    whole = gather_rows(quarter, "grp")

    order = ring_order(count)
    up = [(order[i], order[(i + 1) % count]) for i in range(count)]
    down = [(b, a) for a, b in up]
    worst = arrival(count)
    pool = [scaled]
    ahead = behind = scaled
    for step in range(1, count // 2 + 1):
        if step < count // 2:
            ahead = lax.ppermute(ahead, "blk", up)
            behind = lax.ppermute(behind, "blk", down)
            pool += [ahead, behind]
        else:
            half = scaled.shape[0] // 2
            upper = lax.ppermute(ahead[:half], "blk", up)
            lower = lax.ppermute(behind[half:], "blk", down)
            pool += [jnp.concatenate([upper, lower], axis=0)]

    place = np.zeros(count, np.int32)
    place[order] = np.arange(count)
    place = jnp.asarray(place)
    me = lax.axis_index("blk")
    offset = lax.dynamic_index_in_dim(offsets, lax.axis_index("grp"), 0, keepdims=False)
    block = (me - offset - jnp.arange(STOPS, dtype=jnp.int32)) % count
    back = (place[me] - place[block]) % count
    slot = jnp.where(
        back == 0, 0, jnp.where(back <= count // 2, 2 * back - 1, 2 * (count - back))
    ).astype(jnp.int32)
    rank = jnp.sum((slot[None, :] < slot[:, None]).astype(jnp.int32), axis=1)
    ranked = jnp.sum(
        jnp.where(rank[None, :] == jnp.arange(STOPS)[:, None], slot[None, :], 0), axis=1
    ).astype(jnp.int32)

    total = None
    for first, end in CALLS:
        there = pool[: 2 * worst[end - 1] + 1]
        total = exchange_terms(ranked[first:end], there, whole, total, consts)
    return scatter_rows(total, "grp").reshape(targets.shape)


def solution(mesh):
    in_specs = (P("blk", "grp"), P(("grp", "blk"), None), P(("grp", "blk")), P())
    out_specs = P("blk", "grp")
    return jax.shard_map(local, mesh=mesh, in_specs=in_specs, out_specs=out_specs, check_vma=False)
```
